512 devices in a mesh: ctx: 64 (over x, z, core), head: 8 (over y).
Axes of the slice: x: 4, y: 8, z: 8, core: 2. Of those that a mesh axis runs over, the one named last changes fastest.
Arguments:
- query_rows: bfloat16 [65536, 1024], P('ctx', 'head'), may hold values from -8 to 8
- key_rows: bfloat16 [65536, 1024], P('ctx', 'head'), may hold values from -8 to 8
- value_rows: bfloat16 [65536, 1024], P('ctx', 'head'), may hold values from -6 to 6
- out_grad: bfloat16 [65536, 1024], P('ctx', 'head'), may hold values from -6 to 6
- out_weight: bfloat16 [1024, 1024], P('head'), may hold values from -0.1875 to 0.1875
- neighbours: int32 [512, 12], replicated, may hold values from 0 to 511, as said below
- counts: int32 [512], replicated, may hold values from 3 to 12, as said below
Outputs:
- query_grad: bfloat16 [65536, 1024], P('ctx', 'head')
- key_grad: bfloat16 [65536, 1024], P('ctx', 'head')
- value_grad: bfloat16 [65536, 1024], P('ctx', 'head')
- weight_grad: float32 [1024, 1024], P('head')
The draws below stay inside these ranges and needn't reach their ends.
Inputs may be any that keep to these rules, and one draw needn't show every extreme that they name: `neighbours`: row g names block g in slot 0, then distinct blocks held by ctx indices g // 8 - 1 to g // 8 + 1; slots 1 and 2 include a block of each of the ctx indices g // 8 - 1 and g // 8 + 1 that exists; slots from counts[g] on hold g again. `counts`: block 0 uses all 12 slots.
All inputs are finite; a program needn't handle non-finite values.
Results may differ from the reference program's by a relative error of at most 0.012.
The reference program's roundings to bfloat16 on the way (of `soft_weights`, `attended`, `grad_attended` and `grad_scores`) count: a program that leaves them out, or rounds other values in their place, can miss the bound.
Values may be sent and summed in bfloat16 or wider, within the bound.
No kernel may reach another device: no remote copies, remote signals or barrier semaphores. Data moves between devices by JAX's collectives and lax.ppermute only.
A program may use at most 64 MiB of HBM per device.

```python
import jax
import jax.numpy as jnp
from jax import lax

H = 16
HD = 64
D = 1024
BS = 128
MAXNB = 12
NBD = 8
NBLK = 512
NODES = 65536


def draw_attention_pair(key):
    key = jax.random.fold_in(key, 29)
    queries = jnp.clip(jax.random.normal(jax.random.fold_in(key, 1), (NODES, D), jnp.float32), -6.0, 6.0)
    keys_drawn = jnp.clip(jax.random.normal(jax.random.fold_in(key, 2), (NODES, D), jnp.float32), -6.0, 6.0)
    return (queries, keys_drawn)


def draw_query_rows(key, part):
    return draw_attention_pair(key)[0].astype(jnp.bfloat16)


def draw_key_rows(key, part):
    return draw_attention_pair(key)[1].astype(jnp.bfloat16)


def draw_graph(key):
    key = jax.random.fold_in(key, 17)
    block_ids = jnp.arange(NBLK, dtype=jnp.int32)
    holder = block_ids // NBD
    least = min(3, MAXNB)
    levels = jax.random.randint(jax.random.fold_in(key, 1), (NBLK // NBD,), 0, 4)
    spread = jnp.maximum(1, (MAXNB - least + 1) * (levels + 1) // 4)[holder]
    counts = least + jax.random.randint(jax.random.fold_in(key, 2), (NBLK,), 0, 1 << 20) % spread
    counts = jnp.minimum(counts, MAXNB)
    counts = counts.at[0].set(MAXNB)
    places = jnp.arange(3 * NBD, dtype=jnp.int32)
    candidates = (holder[:, None] - 1) * NBD + places[None, :]
    usable = (candidates >= 0) & (candidates < NBLK) & (candidates != block_ids[:, None])
    jitter = jax.random.randint(jax.random.fold_in(key, 3), (NBLK, 3 * NBD), 0, 2 ** 14)
    lower_group = places < NBD
    upper_group = places >= 2 * NBD
    group_key = jitter * 256 + places[None, :]
    lower_best = jnp.argmin(jnp.where(lower_group[None, :], group_key, 2 ** 30), axis=1)
    upper_best = jnp.argmin(jnp.where(upper_group[None, :], group_key, 2 ** 30), axis=1)
    first_tier = (places[None, :] == lower_best[:, None]) | (places[None, :] == upper_best[:, None])
    tier = jnp.where(usable, jnp.where(first_tier, 0, 1), 2)
    ranking = tier * 2 ** 23 + group_key
    ranked = jnp.argsort(ranking, axis=1, stable=True)[:, :MAXNB - 1]
    picked = jnp.take_along_axis(candidates, ranked, axis=1)
    listed = jnp.concatenate([block_ids[:, None], picked], axis=1)
    slot_ids = jnp.arange(MAXNB, dtype=jnp.int32)
    listed = jnp.where(slot_ids[None, :] < counts[:, None], listed, block_ids[:, None])
    return (listed.astype(jnp.int32), counts.astype(jnp.int32))


def draw_neighbours(key, part):
    return draw_graph(key)[0]


def draw_counts(key, part):
    return draw_graph(key)[1]


def block_scale(key, extent, cuts, low, largest):
    factor_of, own = 1.0, jax.random.fold_in(key, 6)
    for axis_at, parts in cuts:
        draws = jnp.exp(jax.random.uniform(jax.random.fold_in(own, axis_at), (parts,), jnp.float32, low / len(cuts), largest / len(cuts)))
        factor_of = factor_of * jnp.repeat(draws, extent[axis_at] // parts).reshape([-1 if axis == axis_at else 1 for axis in range(len(extent))])
    return factor_of


def gaussian(own_key, extent, scale, reach, split=(), kind=jnp.bfloat16):
    loudness = block_scale(own_key, extent, split, -0.22, 0.18) if split else 1.0
    values = jax.random.normal(own_key, extent, jnp.float32) * scale * loudness
    return jnp.minimum(jnp.maximum(values, -reach), reach).astype(kind)


def setup_inputs(seed: int = 0) -> dict:
    key_of = jax.random.split(jax.random.key(seed), 8)
    return {
        "query_rows": draw_query_rows(jax.random.fold_in(key_of[7], 71), 0),
        "key_rows": draw_key_rows(jax.random.fold_in(key_of[7], 71), 0),
        "value_rows": gaussian(key_of[2], (NODES, D), 1.0, 6.0, ((0, 64), (1, 8))),
        "out_grad": gaussian(key_of[3], (NODES, D), 1.0, 6.0, ((0, 64), (1, 8))),
        "out_weight": gaussian(key_of[4], (D, D), D ** -0.5, 0.1875, ((0, 8),)),
        "neighbours": draw_neighbours(jax.random.fold_in(key_of[7], 71), 0),
        "counts": draw_counts(jax.random.fold_in(key_of[7], 71), 0),
    }


def to_bf16_kept(values):
    return lax.optimization_barrier(values.astype(jnp.bfloat16)).astype(jnp.float32)


def reference(query_rows, key_rows, value_rows, out_grad, out_weight, neighbours, counts):
    factor = HD ** -0.5
    query_blocks = query_rows.reshape(NBLK, BS, H, HD).astype(jnp.float32)
    key_blocks = key_rows.reshape(NBLK, BS, H, HD).astype(jnp.float32)
    value_blocks = value_rows.reshape(NBLK, BS, H, HD).astype(jnp.float32)
    slot_ids = jnp.arange(MAXNB, dtype=jnp.int32)

    def gather_keys(block_index):
        listed = neighbours[block_index]
        usable = slot_ids < counts[block_index]
        key_mask = jnp.repeat(usable, BS)
        picked_keys = key_blocks[listed].reshape(MAXNB * BS, H, HD)
        picked_values = value_blocks[listed].reshape(MAXNB * BS, H, HD)
        return listed, key_mask, picked_keys, picked_values

    def masked_scores(query_block, picked_keys, key_mask):
        scores = jnp.einsum("qhd,khd->hqk", query_block, picked_keys) * factor
        return jnp.where(key_mask[None, None, :], scores, -1e30)

    def forward_block(block_index):
        listed, key_mask, picked_keys, picked_values = gather_keys(block_index)
        scores = masked_scores(query_blocks[block_index], picked_keys, key_mask)
        highest = jnp.max(scores, axis=2)
        log_total = highest + jnp.log(jnp.sum(jnp.exp(scores - highest[:, :, None]), axis=2))
        soft_weights = to_bf16_kept(jnp.exp(scores - log_total[:, :, None]))
        attended = jnp.einsum("hqk,khd->qhd", soft_weights, picked_values)
        return attended.astype(jnp.bfloat16), log_total

    attended_blocks, log_totals = lax.map(forward_block, jnp.arange(NBLK, dtype=jnp.int32))
    attended = attended_blocks.reshape(NODES, D)
    grad_attended = jnp.dot(out_grad, out_weight.T, preferred_element_type=jnp.float32).astype(jnp.bfloat16)
    weight_grad = jnp.dot(attended.T, out_grad, preferred_element_type=jnp.float32) * (NODES ** -0.5)
    grad_blocks = grad_attended.reshape(NBLK, BS, H, HD).astype(jnp.float32)
    row_dots = jnp.sum(grad_blocks * attended_blocks.astype(jnp.float32), axis=3)

    def backward_block(totals, block_index):
        key_total, value_total = totals
        listed, key_mask, picked_keys, picked_values = gather_keys(block_index)
        query_block = query_blocks[block_index]
        grad_block = grad_blocks[block_index]
        scores = masked_scores(query_block, picked_keys, key_mask)
        soft_full = jnp.exp(scores - log_totals[block_index][:, :, None])
        grad_weights = jnp.einsum("qhd,khd->hqk", grad_block, picked_values)
        grad_scores = to_bf16_kept(soft_full * (grad_weights - row_dots[block_index].T[:, :, None]))
        soft_weights = to_bf16_kept(soft_full)
        grad_query = jnp.einsum("hqk,khd->qhd", grad_scores, picked_keys) * factor
        grad_key = jnp.einsum("hqk,qhd->khd", grad_scores, query_block) * factor
        grad_value = jnp.einsum("hqk,qhd->khd", soft_weights, grad_block)
        key_total = key_total.at[listed].add(grad_key.reshape(MAXNB, BS, D))
        value_total = value_total.at[listed].add(grad_value.reshape(MAXNB, BS, D))
        return (key_total, value_total), grad_query.astype(jnp.bfloat16)

    blank_totals = jnp.zeros((NBLK, BS, D), jnp.float32)
    (key_total, value_total), grad_queries = lax.scan(backward_block, (blank_totals, blank_totals), jnp.arange(NBLK, dtype=jnp.int32))
    query_grad = grad_queries.reshape(NODES, D)
    key_grad = key_total.reshape(NODES, D).astype(jnp.bfloat16)
    value_grad = value_total.reshape(NODES, D).astype(jnp.bfloat16)
    return (query_grad, key_grad, value_grad, weight_grad)
```

```python
import jax
import jax.numpy as jnp
from jax import lax
from jax.experimental import pallas as pl
from jax.experimental.pallas import tpu as pltpu
from jax.sharding import PartitionSpec as P

HD = 64
BS = 128
SIZES = (4, 6, 8, 10, 12)


def by_size(active, run):
    low = 0
    for size in SIZES:
        pl.when((active > low) & (active <= size))(lambda size=size: run(size))
        low = size


def spread_columns(rows_t):
    blank = jnp.zeros((HD, BS), rows_t.dtype)
    upper = jnp.concatenate([rows_t[:HD], blank], axis=1)
    lower = jnp.concatenate([blank, rows_t[HD:]], axis=1)
    return jnp.concatenate([upper, lower], axis=0)


def spread_rows(rows):
    lane = lax.broadcasted_iota(jnp.int32, rows.shape, 1)
    blank = jnp.zeros_like(rows)
    return jnp.concatenate(
        [jnp.where(lane < HD, rows, blank), jnp.where(lane >= HD, rows, blank)], axis=0
    )


def own_heads(both):
    return jnp.concatenate([both[:HD, :BS], both[HD:, BS:]], axis=0)


def dot(a, b):
    return jnp.dot(a, b, preferred_element_type=jnp.float32)


def forward_kernel(
    places, active, q_ref, mid_k, mid_v, left, right, att_ref, p_ref, kt_ref, v_ref, k_scr, vt_scr, s_scr
):
    step = pl.program_id(0)
    blocks = pl.num_programs(0)
    factor = HD ** (-0.5)

    @pl.when(step == 0)
    def _():
        count = mid_k.shape[0] // BS
        for b in range(3 * count):
            side, at = divmod(b, count)
            rows = pl.ds(at * BS, BS)
            if side == 1:
                k, v = mid_k[rows, :], mid_v[rows, :]
            else:
                source = left if side == 0 else right
                k, v = source[rows, :BS], source[rows, BS:]
            k_scr[b] = k
            kt_ref[b] = k.T
            v_ref[b] = v
            vt_scr[b] = v.T

    query = spread_columns(q_ref[...].T * factor)

    def run(size):
        highest = None
        for s in range(size):
            scores = dot(k_scr[places[step, s]], query)
            if s == size - 1:
                scores = jnp.where(s < active[step], scores, -1e30)
            s_scr[pl.ds(s * BS, BS), :] = scores
            part = jnp.max(scores.reshape(BS // 8, 8, 2 * BS), axis=0)
            highest = part if highest is None else jnp.maximum(highest, part)
        highest = jnp.max(highest, axis=0, keepdims=True)
        total = None
        for s in range(size):
            grown = jnp.exp(s_scr[pl.ds(s * BS, BS), :] - highest)
            s_scr[pl.ds(s * BS, BS), :] = grown
            part = jnp.sum(grown.reshape(BS // 8, 8, 2 * BS), axis=0)
            total = part if total is None else total + part
        inverse = 1.0 / jnp.sum(total, axis=0, keepdims=True)
        attended = None
        for s in range(size):
            weights = s_scr[pl.ds(s * BS, BS), :] * inverse
            p_ref[0, pl.ds(s * BS, BS), :] = weights
            term = dot(vt_scr[places[step, s]], weights.astype(jnp.bfloat16))
            attended = term if attended is None else attended + term
        att_ref[...] = own_heads(attended).astype(jnp.bfloat16)

    by_size(active[step], run)


def forward(places, active, query_rows, key_rows, value_rows, left, right):
    blocks, slots = places.shape
    rows, cols = query_rows.shape
    extent = 3 * blocks
    whole = lambda *shape: pl.BlockSpec(shape, lambda i, *_: (0,) * len(shape))
    window = jax.ShapeDtypeStruct((extent, BS, cols), jnp.bfloat16)
    return pl.pallas_call(
        forward_kernel,
        grid_spec=pltpu.PrefetchScalarGridSpec(
            num_scalar_prefetch=2,
            grid=(blocks,),
            in_specs=[
                pl.BlockSpec((BS, cols), lambda i, *_: (i, 0)),
                whole(rows, cols),
                whole(rows, cols),
                whole(rows, 2 * cols),
                whole(rows, 2 * cols),
            ],
            out_specs=[
                pl.BlockSpec((cols, BS), lambda i, *_: (0, i)),
                pl.BlockSpec((1, slots * BS, 2 * BS), lambda i, *_: (i, 0, 0)),
                whole(extent, BS, cols),
                whole(extent, BS, cols),
            ],
            scratch_shapes=[
                pltpu.VMEM((extent, BS, cols), jnp.bfloat16),
                pltpu.VMEM((extent, BS, cols), jnp.bfloat16),
                pltpu.VMEM((slots * BS, 2 * BS), jnp.float32),
            ],
        ),
        out_shape=[
            jax.ShapeDtypeStruct((cols, rows), jnp.bfloat16),
            jax.ShapeDtypeStruct((blocks, slots * BS, 2 * BS), jnp.float32),
            window,
            window,
        ],
        compiler_params=pltpu.CompilerParams(dimension_semantics=("arbitrary",)),
        name="forward",
    )(places, active, query_rows, key_rows, value_rows, left, right)


def backward_kernel(
    places, active, q_ref, ga_ref, att_ref, p_ref, kt_ref, v_ref, dq_ref, mid_ref, left_ref, right_ref, dk, dv
):
    step = pl.program_id(0)
    factor = HD ** (-0.5)

    @pl.when(step == 0)
    def _():
        dk[...] = jnp.zeros_like(dk)
        dv[...] = jnp.zeros_like(dv)

    grad = ga_ref[...]
    grad_t = grad.T
    products = grad_t.astype(jnp.float32) * att_ref[...].astype(jnp.float32)
    dots = jnp.concatenate(
        [
            jnp.sum(products[:HD], axis=0, keepdims=True),
            jnp.sum(products[HD:], axis=0, keepdims=True),
        ],
        axis=1,
    )
    grad_wide = spread_columns(grad_t)
    grad_tall = spread_rows(grad)
    query_tall = spread_rows(q_ref[...] * factor)

    def run(size):
        total = None
        for s in range(size):
            place = places[step, s]
            weights = p_ref[0, pl.ds(s * BS, BS), :]
            change = weights * (dot(v_ref[place], grad_wide) - dots)
            change = change.astype(jnp.bfloat16)
            term = dot(kt_ref[place], change)
            total = term if total is None else total + term
            dk[place] += dot(change, query_tall)
            dv[place] += dot(weights.astype(jnp.bfloat16), grad_tall)
        dq_ref[...] = (own_heads(total) * factor).T.astype(jnp.bfloat16)

    by_size(active[step], run)

    @pl.when(step == pl.num_programs(0) - 1)
    def _():
        count = mid_ref.shape[0] // BS
        for b in range(3 * count):
            side, at = divmod(b, count)
            target = (left_ref, mid_ref, right_ref)[side]
            rows = pl.ds(at * BS, BS)
            target[rows, :BS] = dk[b].astype(target.dtype)
            target[rows, BS:] = dv[b].astype(target.dtype)


def backward(places, active, query_rows, grad_attended, att_t, weights, keys_t, values):
    blocks, slots = places.shape
    rows, cols = query_rows.shape
    extent = 3 * blocks
    whole = lambda *shape: pl.BlockSpec(shape, lambda i, *_: (0,) * len(shape))
    one = pl.BlockSpec((BS, cols), lambda i, *_: (i, 0))
    return pl.pallas_call(
        backward_kernel,
        grid_spec=pltpu.PrefetchScalarGridSpec(
            num_scalar_prefetch=2,
            grid=(blocks,),
            in_specs=[
                one,
                one,
                pl.BlockSpec((cols, BS), lambda i, *_: (0, i)),
                pl.BlockSpec((1, slots * BS, 2 * BS), lambda i, *_: (i, 0, 0)),
                whole(extent, BS, cols),
                whole(extent, BS, cols),
            ],
            out_specs=[one, whole(rows, 2 * cols), whole(rows, 2 * cols), whole(rows, 2 * cols)],
            scratch_shapes=[
                pltpu.VMEM((extent, BS, cols), jnp.float32),
                pltpu.VMEM((extent, BS, cols), jnp.float32),
            ],
        ),
        out_shape=[
            jax.ShapeDtypeStruct((rows, cols), jnp.bfloat16),
            jax.ShapeDtypeStruct((rows, 2 * cols), jnp.float32),
            jax.ShapeDtypeStruct((rows, 2 * cols), jnp.bfloat16),
            jax.ShapeDtypeStruct((rows, 2 * cols), jnp.bfloat16),
        ],
        compiler_params=pltpu.CompilerParams(dimension_semantics=("arbitrary",)),
        name="backward",
    )(places, active, query_rows, grad_attended, att_t, weights, keys_t, values)


def shifted(x, axis, by):
    count = lax.axis_size(axis)
    return lax.ppermute(x, axis, [(i, (i + by) % count) for i in range(count)])


def body(query_rows, key_rows, value_rows, out_grad, out_weight, neighbours, counts):
    row_count, col_count = query_rows.shape
    blocks = row_count // BS
    extent = 3 * blocks
    ctx_index = lax.axis_index("ctx")
    packed = jnp.concatenate([key_rows, value_rows], axis=1)
    left = shifted(packed, "ctx", 1)
    right = shifted(packed, "ctx", -1)
    first = ctx_index * blocks
    places = lax.dynamic_slice_in_dim(neighbours, first, blocks, axis=0)
    places = jnp.clip(places - (first - blocks), 0, extent - 1)
    active = lax.dynamic_slice_in_dim(counts, first, blocks, axis=0)
    att_t, weights, keys_t, values = forward(
        places, active, query_rows, key_rows, value_rows, left, right
    )
    gathered = lax.all_gather(out_grad, "head", axis=1, tiled=True)
    grad_attended = jnp.einsum(
        "ro,jo->rj", gathered, out_weight, preferred_element_type=jnp.float32
    ).astype(jnp.bfloat16)
    product = jnp.einsum("jr,ro->jo", att_t, gathered, preferred_element_type=jnp.float32)
    node_count = row_count * lax.axis_size("ctx")
    weight_grad = lax.psum(product, "ctx") * node_count ** (-0.5)
    query_grad, middle, to_left, to_right = backward(
        places, active, query_rows, grad_attended, att_t, weights, keys_t, values
    )
    from_right = shifted(to_left, "ctx", -1)
    from_left = shifted(to_right, "ctx", 1)
    combined = middle + from_right.astype(jnp.float32) + from_left.astype(jnp.float32)
    key_grad = combined[:, :col_count].astype(jnp.bfloat16)
    value_grad = combined[:, col_count:].astype(jnp.bfloat16)
    return (query_grad, key_grad, value_grad, weight_grad)


def solution(mesh):
    placed = (
        P("ctx", "head"),
        P("ctx", "head"),
        P("ctx", "head"),
        P("ctx", "head"),
        P("head", None),
        P(),
        P(),
    )
    return jax.shard_map(
        body,
        mesh=mesh,
        in_specs=placed,
        out_specs=(P("ctx", "head"), P("ctx", "head"), P("ctx", "head"), P("head", None)),
        check_vma=False,
    )
```

```python
import jax
import jax.numpy as jnp
from jax import lax
from jax.experimental import pallas as pl
from jax.experimental.pallas import tpu as pltpu
from jax.sharding import PartitionSpec as P

HD = 64
BS = 128
SIZES = (4, 6, 8, 10, 12)


def by_size(active, run):
    low = 0
    for size in SIZES:
        pl.when((active > low) & (active <= size))(lambda size=size: run(size))
        low = size


def spread_columns(rows_t):
    blank = jnp.zeros((HD, BS), rows_t.dtype)
    upper = jnp.concatenate([rows_t[:HD], blank], axis=1)
    lower = jnp.concatenate([blank, rows_t[HD:]], axis=1)
    return jnp.concatenate([upper, lower], axis=0)


def spread_rows(rows):
    lane = lax.broadcasted_iota(jnp.int32, rows.shape, 1)
    blank = jnp.zeros_like(rows)
    return jnp.concatenate(
        [jnp.where(lane < HD, rows, blank), jnp.where(lane >= HD, rows, blank)], axis=0
    )


def own_heads(both):
    return jnp.concatenate([both[:HD, :BS], both[HD:, BS:]], axis=0)


def dot(a, b):
    return jnp.dot(a, b, preferred_element_type=jnp.float32)


def forward_kernel(
    places, active, q_ref, mid_k, mid_v, left, right, att_ref, p_ref, kt_ref, v_ref, k_scr, vt_scr, s_scr
):
    step = pl.program_id(0)
    blocks = pl.num_programs(0)
    factor = HD ** (-0.5)

    @pl.when(step == 0)
    def _():
        count = mid_k.shape[0] // BS
        for b in range(3 * count):
            side, at = divmod(b, count)
            rows = pl.ds(at * BS, BS)
            if side == 1:
                k, v = mid_k[rows, :], mid_v[rows, :]
            else:
                source = left if side == 0 else right
                k, v = source[rows, :BS], source[rows, BS:]
            k_scr[b] = k
            kt_ref[b] = k.T
            v_ref[b] = v
            vt_scr[b] = v.T

    query = spread_columns(q_ref[...].T * factor)

    def run(size):
        highest = None
        for s in range(size):
            scores = dot(k_scr[places[step, s]], query)
            if s == size - 1:
                scores = jnp.where(s < active[step], scores, -1e30)
            s_scr[pl.ds(s * BS, BS), :] = scores
            part = jnp.max(scores.reshape(BS // 8, 8, 2 * BS), axis=0)
            highest = part if highest is None else jnp.maximum(highest, part)
        highest = jnp.max(highest, axis=0, keepdims=True)
        total = None
        for s in range(size):
            grown = jnp.exp(s_scr[pl.ds(s * BS, BS), :] - highest)
            s_scr[pl.ds(s * BS, BS), :] = grown
            part = jnp.sum(grown.reshape(BS // 8, 8, 2 * BS), axis=0)
            total = part if total is None else total + part
        inverse = 1.0 / jnp.sum(total, axis=0, keepdims=True)
        attended = None
        for s in range(size):
            weights = s_scr[pl.ds(s * BS, BS), :] * inverse
            p_ref[0, pl.ds(s * BS, BS), :] = weights
            term = dot(vt_scr[places[step, s]], weights.astype(jnp.bfloat16))
            attended = term if attended is None else attended + term
        att_ref[...] = own_heads(attended).astype(jnp.bfloat16)

    by_size(active[step], run)


def forward(places, active, query_rows, key_rows, value_rows, left, right):
    blocks, slots = places.shape
    rows, cols = query_rows.shape
    extent = 3 * blocks
    whole = lambda *shape: pl.BlockSpec(shape, lambda i, *_: (0,) * len(shape))
    window = jax.ShapeDtypeStruct((extent, BS, cols), jnp.bfloat16)
    return pl.pallas_call(
        forward_kernel,
        grid_spec=pltpu.PrefetchScalarGridSpec(
            num_scalar_prefetch=2,
            grid=(blocks,),
            in_specs=[
                pl.BlockSpec((BS, cols), lambda i, *_: (i, 0)),
                whole(rows, cols),
                whole(rows, cols),
                whole(rows, 2 * cols),
                whole(rows, 2 * cols),
            ],
            out_specs=[
                pl.BlockSpec((cols, BS), lambda i, *_: (0, i)),
                pl.BlockSpec((1, slots * BS, 2 * BS), lambda i, *_: (i, 0, 0)),
                whole(extent, BS, cols),
                whole(extent, BS, cols),
            ],
            scratch_shapes=[
                pltpu.VMEM((extent, BS, cols), jnp.bfloat16),
                pltpu.VMEM((extent, BS, cols), jnp.bfloat16),
                pltpu.VMEM((slots * BS, 2 * BS), jnp.float32),
            ],
        ),
        out_shape=[
            jax.ShapeDtypeStruct((cols, rows), jnp.bfloat16),
            jax.ShapeDtypeStruct((blocks, slots * BS, 2 * BS), jnp.float32),
            window,
            window,
        ],
        compiler_params=pltpu.CompilerParams(dimension_semantics=("arbitrary",)),
        name="forward",
    )(places, active, query_rows, key_rows, value_rows, left, right)


def backward_kernel(
    places, active, q_ref, ga_ref, att_ref, p_ref, kt_ref, v_ref, dq_ref, mid_ref, left_ref, right_ref, dk, dv
):
    step = pl.program_id(0)
    factor = HD ** (-0.5)

    @pl.when(step == 0)
    def _():
        dk[...] = jnp.zeros_like(dk)
        dv[...] = jnp.zeros_like(dv)

    grad = ga_ref[...]
    grad_t = grad.T
    products = grad_t.astype(jnp.float32) * att_ref[...].astype(jnp.float32)
    dots = jnp.concatenate(
        [
            jnp.sum(products[:HD], axis=0, keepdims=True),
            jnp.sum(products[HD:], axis=0, keepdims=True),
        ],
        axis=1,
    )
    grad_wide = spread_columns(grad_t)
    grad_tall = spread_rows(grad)
    query_tall = spread_rows(q_ref[...] * factor)

    def run(size):
        total = None
        for s in range(size):
            place = places[step, s]
            weights = p_ref[0, pl.ds(s * BS, BS), :]
            change = weights * (dot(v_ref[place], grad_wide) - dots)
            change = change.astype(jnp.bfloat16)
            term = dot(kt_ref[place], change)
            total = term if total is None else total + term
            dk[place] += dot(change, query_tall)
            dv[place] += dot(weights.astype(jnp.bfloat16), grad_tall)
        dq_ref[...] = (own_heads(total) * factor).T.astype(jnp.bfloat16)

    by_size(active[step], run)

    @pl.when(step == pl.num_programs(0) - 1)
    def _():
        count = mid_ref.shape[0] // BS
        for b in range(3 * count):
            side, at = divmod(b, count)
            target = (left_ref, mid_ref, right_ref)[side]
            rows = pl.ds(at * BS, BS)
            target[rows, :BS] = dk[b].astype(target.dtype)
            target[rows, BS:] = dv[b].astype(target.dtype)


def backward(places, active, query_rows, grad_attended, att_t, weights, keys_t, values):
    blocks, slots = places.shape
    rows, cols = query_rows.shape
    extent = 3 * blocks
    whole = lambda *shape: pl.BlockSpec(shape, lambda i, *_: (0,) * len(shape))
    one = pl.BlockSpec((BS, cols), lambda i, *_: (i, 0))
    return pl.pallas_call(
        backward_kernel,
        grid_spec=pltpu.PrefetchScalarGridSpec(
            num_scalar_prefetch=2,
            grid=(blocks,),
            in_specs=[
                one,
                one,
                pl.BlockSpec((cols, BS), lambda i, *_: (0, i)),
                pl.BlockSpec((1, slots * BS, 2 * BS), lambda i, *_: (i, 0, 0)),
                whole(extent, BS, cols),
                whole(extent, BS, cols),
            ],
            out_specs=[one, whole(rows, 2 * cols), whole(rows, 2 * cols), whole(rows, 2 * cols)],
            scratch_shapes=[
                pltpu.VMEM((extent, BS, cols), jnp.float32),
                pltpu.VMEM((extent, BS, cols), jnp.float32),
            ],
        ),
        out_shape=[
            jax.ShapeDtypeStruct((rows, cols), jnp.bfloat16),
            jax.ShapeDtypeStruct((rows, 2 * cols), jnp.float32),
            jax.ShapeDtypeStruct((rows, 2 * cols), jnp.bfloat16),
            jax.ShapeDtypeStruct((rows, 2 * cols), jnp.bfloat16),
        ],
        compiler_params=pltpu.CompilerParams(dimension_semantics=("arbitrary",)),
        name="backward",
    )(places, active, query_rows, grad_attended, att_t, weights, keys_t, values)


def shifted(x, axis, by):
    count = lax.axis_size(axis)
    return lax.ppermute(x, axis, [(i, (i + by) % count) for i in range(count)])


def project_kernel(head, own, r1, l1, r2, l2, r3, l3, upper, lower, w_ref, att_ref, ga_ref, wg_ref):
    count = wg_ref.shape[0]
    half = upper.shape[0]
    chunks = {0: own, -1: r1, 1: l1, -2: r2, 2: l2, -3: r3, 3: l3}
    att = att_ref[...]
    total = None
    for first, second in ((0, 1), (-1, 2), (-2, 3), (-3, 4)):
        sides, parts = [], []
        for k in (first, second):
            at = lax.rem(head[0] + k + count, count)
            sides.append(w_ref[:, pl.ds(pl.multiple_of(at * BS, BS), BS)])
            if k == 4:
                parts.append(jnp.concatenate([upper[...], lower[...]], axis=0))
            else:
                parts.append(chunks[k][...])
        side = jnp.concatenate(sides, axis=1)
        part = jnp.concatenate(parts, axis=1)
        term = lax.dot_general(
            part, side, (((1,), (1,)), ((), ())), preferred_element_type=jnp.float32
        )
        total = term if total is None else total + term
        grad = dot(att, part)
        wg_ref[first % count] = grad[:, :BS].astype(wg_ref.dtype)
        wg_ref[second % count] = grad[:, BS:].astype(wg_ref.dtype)
    ga_ref[...] = total.astype(jnp.bfloat16)


def project(head, parts, out_weight, att_t):
    rows = parts[0].shape[0]
    cols, width = out_weight.shape
    return pl.pallas_call(
        project_kernel,
        in_specs=[pl.BlockSpec(memory_space=pltpu.SMEM)]
        + [pl.BlockSpec(memory_space=pltpu.VMEM)] * (len(parts) + 2),
        out_shape=[
            jax.ShapeDtypeStruct((rows, cols), jnp.bfloat16),
            jax.ShapeDtypeStruct((width // BS, cols, BS), jnp.bfloat16),
        ],
        name="project",
    )(head, *parts, out_weight, att_t)


def place_kernel(head, sum_ref, out_ref):
    count = sum_ref.shape[0]
    for k in range(count):
        at = lax.rem(head[0] + k, count)
        out_ref[:, pl.ds(pl.multiple_of(at * BS, BS), BS)] = sum_ref[k].astype(jnp.float32)


def place(head, sums):
    count, cols, width = sums.shape
    return pl.pallas_call(
        place_kernel,
        in_specs=[pl.BlockSpec(memory_space=pltpu.SMEM), pl.BlockSpec(memory_space=pltpu.VMEM)],
        out_shape=jax.ShapeDtypeStruct((cols, count * width), jnp.float32),
        name="place",
    )(head, sums)


def head_ring(own):
    half = own.shape[0] // 2
    parts = [own]
    r, l = own, own
    for _ in range(3):
        r, l = shifted(r, "head", 1), shifted(l, "head", -1)
        parts += [r, l]
    parts += [shifted(r[:half], "head", 1), shifted(l[half:], "head", -1)]
    return parts


def total_over(partial, axis, scale):
    members = lax.axis_size(axis)
    shape = partial.shape
    pieces = partial.reshape(members, -1, shape[-1])
    pieces = lax.all_to_all(pieces, axis, 0, 0)
    piece = jnp.sum(pieces.astype(jnp.float32), axis=0) * scale
    piece = piece.astype(partial.dtype)
    pieces = lax.all_to_all(jnp.broadcast_to(piece[None], pieces.shape), axis, 0, 0)
    return pieces.reshape(shape)


def body(query_rows, key_rows, value_rows, out_grad, out_weight, neighbours, counts):
    row_count, col_count = query_rows.shape
    blocks = row_count // BS
    extent = 3 * blocks
    ctx_index = lax.axis_index("ctx")
    packed = jnp.concatenate([key_rows, value_rows], axis=1)
    left = shifted(packed, "ctx", 1)
    right = shifted(packed, "ctx", -1)
    first = ctx_index * blocks
    places = lax.dynamic_slice_in_dim(neighbours, first, blocks, axis=0)
    places = jnp.clip(places - (first - blocks), 0, extent - 1)
    active = lax.dynamic_slice_in_dim(counts, first, blocks, axis=0)
    att_t, weights, keys_t, values = forward(
        places, active, query_rows, key_rows, value_rows, left, right
    )
    head = lax.axis_index("head").reshape(1)
    grad_attended, partial = project(head, head_ring(out_grad), out_weight, att_t)
    node_count = row_count * lax.axis_size("ctx")
    query_grad, middle, to_left, to_right = backward(
        places, active, query_rows, grad_attended, att_t, weights, keys_t, values
    )
    from_right = shifted(to_left, "ctx", -1)
    from_left = shifted(to_right, "ctx", 1)
    weight_sum = total_over(partial, "ctx", node_count ** (-0.5))
    weight_grad = place(head, weight_sum)
    combined = middle + from_right.astype(jnp.float32) + from_left.astype(jnp.float32)
    key_grad = combined[:, :col_count].astype(jnp.bfloat16)
    value_grad = combined[:, col_count:].astype(jnp.bfloat16)
    return (query_grad, key_grad, value_grad, weight_grad)


def solution(mesh):
    placed = (
        P("ctx", "head"),
        P("ctx", "head"),
        P("ctx", "head"),
        P("ctx", "head"),
        P("head", None),
        P(),
        P(),
    )
    return jax.shard_map(
        body,
        mesh=mesh,
        in_specs=placed,
        out_specs=(P("ctx", "head"), P("ctx", "head"), P("ctx", "head"), P("head", None)),
        check_vma=False,
    )
```

```python
import functools

import jax
import jax.numpy as jnp
from jax import lax
from jax.experimental import pallas as pl
from jax.experimental.pallas import tpu as pltpu
from jax.sharding import PartitionSpec as P


HD = 64
BS = 128
SIZES = (4, 6, 8, 10, 12)


def by_size(active, run):
    low = 0
    for size in SIZES:
        pl.when((active > low) & (active <= size))(lambda size=size: run(size))
        low = size


def cost(steps):
    return pl.CostEstimate(flops=2 * steps * 10**9, bytes_accessed=steps * 10**6, transcendentals=0)


def spread_columns(rows_t):
    blank = jnp.zeros((HD, BS), rows_t.dtype)
    upper = jnp.concatenate([rows_t[:HD], blank], axis=1)
    lower = jnp.concatenate([blank, rows_t[HD:]], axis=1)
    return jnp.concatenate([upper, lower], axis=0)


def spread_rows(rows):
    lane = lax.broadcasted_iota(jnp.int32, rows.shape, 1)
    blank = jnp.zeros_like(rows)
    return jnp.concatenate(
        [jnp.where(lane < HD, rows, blank), jnp.where(lane >= HD, rows, blank)], axis=0
    )


def own_heads(both):
    return jnp.concatenate([both[:HD, :BS], both[HD:, BS:]], axis=0)


def dot(a, b):
    return jnp.dot(a, b, preferred_element_type=jnp.float32)


def forward_kernel(skip, places, active, q_ref, *rest):
    factor = HD ** (-0.5)
    if skip:
        (k_ref, vt_ref, _, _, att_ref, p_ref, s_scr) = rest
    else:
        (mid_k, mid_v, left, right, att_ref, p_ref, kt_ref, v_ref, k_ref, vt_ref, s_scr) = rest

        @pl.when(pl.program_id(0) == 0)
        def _():
            count = mid_k.shape[0] // BS
            for b in range(3 * count):
                side, at = divmod(b, count)
                rows = pl.ds(at * BS, BS)
                if side == 1:
                    k, v = mid_k[rows, :], mid_v[rows, :]
                else:
                    source = left if side == 0 else right
                    k, v = source[rows, :BS], source[rows, BS:]
                k_ref[b] = k
                kt_ref[b] = k.T
                v_ref[b] = v
                vt_ref[b] = v.T

    step = pl.program_id(0) + skip
    query = spread_columns(q_ref[...].T * factor)

    def run(size):
        highest = None
        for s in range(size):
            scores = dot(k_ref[places[step, s]], query)
            if s == size - 1:
                scores = jnp.where(s < active[step], scores, -1e30)
            s_scr[pl.ds(s * BS, BS), :] = scores
            part = jnp.max(scores.reshape(BS // 8, 8, 2 * BS), axis=0)
            highest = part if highest is None else jnp.maximum(highest, part)
        highest = jnp.max(highest, axis=0, keepdims=True)
        total = None
        for s in range(size):
            grown = jnp.exp(s_scr[pl.ds(s * BS, BS), :] - highest)
            s_scr[pl.ds(s * BS, BS), :] = grown
            part = jnp.sum(grown.reshape(BS // 8, 8, 2 * BS), axis=0)
            total = part if total is None else total + part
        inverse = 1.0 / jnp.sum(total, axis=0, keepdims=True)
        attended = None
        for s in range(0, size, 2):
            weights = s_scr[pl.ds(s * BS, 2 * BS), :] * inverse
            p_ref[0, pl.ds(s * BS, 2 * BS), :] = weights
            pair = jnp.concatenate([vt_ref[places[step, s]], vt_ref[places[step, s + 1]]], axis=1)
            term = dot(pair, weights.astype(jnp.bfloat16))
            attended = term if attended is None else attended + term
        att_ref[...] = own_heads(attended).astype(jnp.bfloat16)

    by_size(active[step], run)


def forward(places, active, query_rows, skip, steps, sources, carried):
    blocks, slots = places.shape
    rows, cols = query_rows.shape
    extent = 3 * blocks
    whole = lambda *shape: pl.BlockSpec(shape, lambda i, *_: (0,) * len(shape))
    window = jax.ShapeDtypeStruct((extent, BS, cols), jnp.bfloat16)
    count = 0 if skip else 4
    in_specs = [pl.BlockSpec((BS, cols), lambda i, *_: (i + skip, 0))]
    in_specs += [whole(*x.shape) for x in sources]
    in_specs += [pl.BlockSpec(memory_space=pl.ANY)] * len(carried)
    return pl.pallas_call(
        functools.partial(forward_kernel, skip),
        grid_spec=pltpu.PrefetchScalarGridSpec(
            num_scalar_prefetch=2,
            grid=(steps,),
            in_specs=in_specs,
            out_specs=[
                pl.BlockSpec((cols, BS), lambda i, *_: (0, i + skip)),
                pl.BlockSpec((1, slots * BS, 2 * BS), lambda i, *_: (i + skip, 0, 0)),
            ]
            + [whole(extent, BS, cols)] * count,
            scratch_shapes=[pltpu.VMEM((slots * BS, 2 * BS), jnp.float32)],
        ),
        out_shape=[
            jax.ShapeDtypeStruct((cols, rows), jnp.bfloat16),
            jax.ShapeDtypeStruct((blocks, slots * BS, 2 * BS), jnp.float32),
        ]
        + [window] * count,
        input_output_aliases={5: 0, 6: 1} if skip else {},
        compiler_params=pltpu.CompilerParams(dimension_semantics=("arbitrary",)),
        cost_estimate=cost(steps),
        name="forward",
    )(places, active, query_rows, *sources, *carried)


def backward_kernel(first, last, places, active, q_ref, ga_ref, att_ref, p_ref, kt_ref, v_ref, *rest):
    if first:
        (dq_ref, dk, dv) = rest
    elif last:
        (_, dk_base, dv_base, dq_ref, mid_ref, left_ref, right_ref, dk, dv) = rest
    here = pl.program_id(0)
    factor = HD ** (-0.5)

    @pl.when(here == 0)
    def _():
        if first:
            dk[...] = jnp.zeros_like(dk)
            dv[...] = jnp.zeros_like(dv)
        else:
            dk[...] = dk_base[...]
            dv[...] = dv_base[...]

    step = here if first else here + pl.num_programs(0)
    grad = ga_ref[...]
    grad_t = grad.T
    products = grad_t.astype(jnp.float32) * att_ref[...].astype(jnp.float32)
    dots = jnp.concatenate(
        [
            jnp.sum(products[:HD], axis=0, keepdims=True),
            jnp.sum(products[HD:], axis=0, keepdims=True),
        ],
        axis=1,
    )
    grad_wide = spread_columns(grad_t)
    grad_tall = spread_rows(grad)
    query_tall = spread_rows(q_ref[...] * factor)

    def run(size):
        total = None
        for s in range(0, size, 2):
            changes, pair = [], []
            for j in range(2):
                place = places[step, s + j]
                weights = p_ref[0, pl.ds((s + j) * BS, BS), :]
                change = weights * (dot(v_ref[place], grad_wide) - dots)
                change = change.astype(jnp.bfloat16)
                changes.append(change)
                pair.append(kt_ref[place])
                dk[place] += dot(change, query_tall)
                dv[place] += dot(weights.astype(jnp.bfloat16), grad_tall)
            term = dot(jnp.concatenate(pair, axis=1), jnp.concatenate(changes, axis=0))
            total = term if total is None else total + term
        dq_ref[...] = (own_heads(total) * factor).T.astype(jnp.bfloat16)

    by_size(active[step], run)

    if last:

        @pl.when(here == pl.num_programs(0) - 1)
        def _():
            count = mid_ref.shape[0] // BS
            for b in range(3 * count):
                side, at = divmod(b, count)
                target = (left_ref, mid_ref, right_ref)[side]
                rows = pl.ds(at * BS, BS)
                target[rows, :BS] = dk[b].astype(target.dtype)
                target[rows, BS:] = dv[b].astype(target.dtype)


def backward(places, active, query_rows, grad_attended, att_t, weights, keys_t, values, base):
    blocks, slots = places.shape
    rows, cols = query_rows.shape
    extent = 3 * blocks
    steps = blocks // 2
    first = not base
    skip = 0 if first else steps
    whole = lambda *shape: pl.BlockSpec(shape, lambda i, *_: (0,) * len(shape))
    one = pl.BlockSpec((BS, cols), lambda i, *_: (i + skip, 0))
    sums = jax.ShapeDtypeStruct((extent, BS, cols), jnp.float32)
    in_specs = [
        one,
        one,
        pl.BlockSpec((cols, BS), lambda i, *_: (0, i + skip)),
        pl.BlockSpec((1, slots * BS, 2 * BS), lambda i, *_: (i + skip, 0, 0)),
        whole(extent, BS, cols),
        whole(extent, BS, cols),
    ]
    out_shape = [jax.ShapeDtypeStruct((rows, cols), jnp.bfloat16)]
    if first:
        out_specs = [one, whole(*sums.shape), whole(*sums.shape)]
        out_shape += [sums, sums]
        scratch, aliases = [], {}
    else:
        in_specs += [pl.BlockSpec(memory_space=pl.ANY), whole(*sums.shape), whole(*sums.shape)]
        out_specs = [one] + [whole(rows, 2 * cols)] * 3
        out_shape += [
            jax.ShapeDtypeStruct((rows, 2 * cols), kind)
            for kind in (jnp.float32, jnp.bfloat16, jnp.bfloat16)
        ]
        scratch = [pltpu.VMEM(sums.shape, jnp.float32)] * 2
        aliases = {len(in_specs) - 3 + 2: 0}
    return pl.pallas_call(
        functools.partial(backward_kernel, first, not first),
        grid_spec=pltpu.PrefetchScalarGridSpec(
            num_scalar_prefetch=2,
            grid=(steps,),
            in_specs=in_specs,
            out_specs=out_specs,
            scratch_shapes=scratch,
        ),
        out_shape=out_shape,
        input_output_aliases=aliases,
        compiler_params=pltpu.CompilerParams(dimension_semantics=("arbitrary",)),
        cost_estimate=cost(2 * steps),
        name="backward",
    )(places, active, query_rows, grad_attended, att_t, weights, keys_t, values, *base)


def shifted(x, axis, by):
    count = lax.axis_size(axis)
    return lax.ppermute(x, axis, [(i, (i + by) % count) for i in range(count)])


def project_kernel(skip, order, *refs):
    w_ref, att_ref = refs[:2]
    ga_ref, wg_ref = refs[-2:]
    chunks = refs[2:-2]
    total = None
    if skip:
        total = chunks[0][...]
        wg_ref[...] = chunks[1][...]
        chunks = chunks[2:]
    att = att_ref[...]
    for k in range(0, len(chunks), 2):
        places = [order[skip + k + j] for j in range(2)]
        part = jnp.concatenate([chunks[k][...], chunks[k + 1][...]], axis=1)
        sides = [w_ref[:, pl.ds(pl.multiple_of(at * BS, BS), BS)] for at in places]
        term = lax.dot_general(
            part,
            jnp.concatenate(sides, axis=1),
            (((1,), (1,)), ((), ())),
            preferred_element_type=jnp.float32,
        )
        total = term if total is None else total + term
        grad = dot(att, part)
        for j in range(2):
            wg_ref[places[j]] = grad[:, j * BS : (j + 1) * BS].astype(wg_ref.dtype)
    ga_ref[...] = total.astype(ga_ref.dtype)


def project(order, chunks, out_weight, att_t, base):
    rows = chunks[0].shape[0]
    cols, width = out_weight.shape
    count = width // BS
    return pl.pallas_call(
        functools.partial(project_kernel, count - len(chunks) if base else 0),
        in_specs=[pl.BlockSpec(memory_space=pltpu.SMEM)]
        + [pl.BlockSpec(memory_space=pltpu.VMEM)] * (len(chunks) + len(base) + 2),
        out_shape=[
            jax.ShapeDtypeStruct((rows, cols), jnp.bfloat16 if base else jnp.float32),
            jax.ShapeDtypeStruct((count, cols, BS), jnp.bfloat16),
        ],
        cost_estimate=cost(1),
        name="project",
    )(order, out_weight, att_t, *base, *chunks)


def place_kernel(sum_ref, out_ref):
    for k in range(sum_ref.shape[0]):
        out_ref[:, k * BS : (k + 1) * BS] = sum_ref[k].astype(jnp.float32)


def place(sums):
    count, cols, width = sums.shape
    return pl.pallas_call(
        place_kernel,
        out_shape=jax.ShapeDtypeStruct((cols, count * width), jnp.float32),
        name="place",
    )(sums)


def next_head(x):
    rings, count = lax.axis_size("ctx"), lax.axis_size("head")
    pairs = []
    for c in range(rings):
        by = 1 - 2 * (c % 2)
        pairs += [(c * count + h, c * count + (h + by) % count) for h in range(count)]
    return lax.ppermute(x, ("ctx", "head"), pairs)


def total_piece(partial, axis, scale):
    members = lax.axis_size(axis)
    pieces = partial.reshape(members, -1, partial.shape[-1])
    pieces = lax.all_to_all(pieces, axis, 0, 0)
    piece = jnp.sum(pieces.astype(jnp.float32), axis=0) * scale
    copies = jnp.broadcast_to(piece.astype(partial.dtype)[None], pieces.shape)
    return copies


def ring_order():
    count = lax.axis_size("head")
    by = 1 - 2 * (lax.axis_index("ctx") % 2)
    return (lax.axis_index("head") - by * jnp.arange(count, dtype=jnp.int32)) % count


def body(query_rows, key_rows, value_rows, out_grad, out_weight, neighbours, counts):
    row_count, col_count = query_rows.shape
    blocks = row_count // BS
    extent = 3 * blocks
    ctx_index = lax.axis_index("ctx")
    packed = jnp.concatenate([key_rows, value_rows], axis=1)
    left = shifted(packed, "ctx", 1)
    right = shifted(packed, "ctx", -1)
    first = ctx_index * blocks
    places = lax.dynamic_slice_in_dim(neighbours, first, blocks, axis=0)
    places = jnp.clip(places - (first - blocks), 0, extent - 1)
    active = lax.dynamic_slice_in_dim(counts, first, blocks, axis=0)
    order = ring_order()
    chunks = [out_grad]
    for _ in range(2):
        chunks.append(next_head(chunks[-1]))
    sources, carried = (key_rows, value_rows, left, right), ()
    for at in range(0, blocks, 2):
        chunks.append(next_head(chunks[-1]))
        outs = forward(places, active, query_rows, at, 2, sources, carried)
        att_t, weights = outs[:2]
        chunks[-1], att_t = lax.optimization_barrier((chunks[-1], att_t))
        if at == 0:
            keys_t, values, *sources = outs[2:]
        carried = (att_t, weights)
    last = next_head(chunks[-1])
    base = project(order, chunks[:6], out_weight, att_t, ())
    last, *base = lax.optimization_barrier((last, *base))
    grad_attended, partial = project(order, [chunks[6], last], out_weight, att_t, base)
    node_count = row_count * lax.axis_size("ctx")
    shared = (att_t, weights, keys_t, values)
    carried = backward(places, active, query_rows, grad_attended, *shared, ())
    copies = total_piece(partial, "ctx", node_count ** (-0.5))
    copies, *carried = lax.optimization_barrier((copies, *carried))
    query_grad, middle, to_left, to_right = backward(
        places, active, query_rows, grad_attended, *shared, carried
    )
    from_right = shifted(to_left, "ctx", -1)
    from_left = shifted(to_right, "ctx", 1)
    weight_sum = lax.all_to_all(copies, "ctx", 0, 0)
    weight_grad = place(weight_sum.reshape(partial.shape))
    combined = middle + from_right.astype(jnp.float32) + from_left.astype(jnp.float32)
    key_grad = combined[:, :col_count].astype(jnp.bfloat16)
    value_grad = combined[:, col_count:].astype(jnp.bfloat16)
    return (query_grad, key_grad, value_grad, weight_grad)


def solution(mesh):
    placed = (
        P("ctx", "head"),
        P("ctx", "head"),
        P("ctx", "head"),
        P("ctx", "head"),
        P("head", None),
        P(),
        P(),
    )
    return jax.shard_map(
        body,
        mesh=mesh,
        in_specs=placed,
        out_specs=(P("ctx", "head"), P("ctx", "head"), P("ctx", "head"), P("head", None)),
        check_vma=False,
    )
```

```python
import functools

import jax
import jax.numpy as jnp
from jax import lax
from jax.experimental import pallas as pl
from jax.experimental.pallas import tpu as pltpu
from jax.sharding import PartitionSpec as P


HD = 64
BS = 128
SIZES = (2, 4, 6, 8, 10, 12)


def by_size(active, run):
    low = -1
    for size in SIZES:
        pl.when((active > low) & (active <= size))(lambda size=size: run(size))
        low = size


def cost(steps):
    return pl.CostEstimate(flops=2 * steps * 10**9, bytes_accessed=steps * 10**6, transcendentals=0)


def spread_columns(rows_t):
    blank = jnp.zeros((HD, BS), rows_t.dtype)
    upper = jnp.concatenate([rows_t[:HD], blank], axis=1)
    lower = jnp.concatenate([blank, rows_t[HD:]], axis=1)
    return jnp.concatenate([upper, lower], axis=0)


def spread_rows(rows):
    lane = lax.broadcasted_iota(jnp.int32, rows.shape, 1)
    blank = jnp.zeros_like(rows)
    return jnp.concatenate(
        [jnp.where(lane < HD, rows, blank), jnp.where(lane >= HD, rows, blank)], axis=0
    )


def own_heads(both):
    return jnp.concatenate([both[:HD, :BS], both[HD:, BS:]], axis=0)


def dot(a, b):
    return jnp.dot(a, b, preferred_element_type=jnp.float32)


def forward_kernel(
    places, active, q_ref, mid_k, mid_v, left, right, att_ref, p_ref, kt_ref, v_ref, k_scr, vt_scr, s_scr
):
    step = pl.program_id(0)
    factor = HD ** (-0.5)

    @pl.when(step == 0)
    def _():
        count = mid_k.shape[0] // BS
        for b in range(3 * count):
            side, at = divmod(b, count)
            rows = pl.ds(at * BS, BS)
            if side == 1:
                k, v = mid_k[rows, :], mid_v[rows, :]
            else:
                source = left if side == 0 else right
                k, v = source[rows, :BS], source[rows, BS:]
            k_scr[b] = k
            kt_ref[b] = k.T
            v_ref[b] = v
            vt_scr[b] = v.T

    query = spread_columns(q_ref[...].T * factor)

    def run(size):
        highest = None
        for s in range(size):
            scores = dot(k_scr[places[step, s]], query)
            if s == size - 1:
                scores = jnp.where(s < active[step], scores, -1e30)
            s_scr[pl.ds(s * BS, BS), :] = scores
            part = jnp.max(scores.reshape(BS // 8, 8, 2 * BS), axis=0)
            highest = part if highest is None else jnp.maximum(highest, part)
        highest = jnp.max(highest, axis=0, keepdims=True)
        total = None
        for s in range(size):
            grown = jnp.exp(s_scr[pl.ds(s * BS, BS), :] - highest)
            s_scr[pl.ds(s * BS, BS), :] = grown
            part = jnp.sum(grown.reshape(BS // 8, 8, 2 * BS), axis=0)
            total = part if total is None else total + part
        inverse = 1.0 / jnp.sum(total, axis=0, keepdims=True)
        attended = None
        for s in range(0, size, 2):
            weights = s_scr[pl.ds(s * BS, 2 * BS), :] * inverse
            p_ref[0, pl.ds(s * BS, 2 * BS), :] = weights
            pair = jnp.concatenate([vt_scr[places[step, s]], vt_scr[places[step, s + 1]]], axis=1)
            term = dot(pair, weights.astype(jnp.bfloat16))
            attended = term if attended is None else attended + term
        att_ref[...] = own_heads(attended).astype(jnp.bfloat16)

    by_size(active[step], run)


def forward(places, active, query_rows, key_rows, value_rows, left, right):
    blocks, slots = places.shape
    rows, cols = query_rows.shape
    extent = 3 * blocks
    whole = lambda *shape: pl.BlockSpec(shape, lambda i, *_: (0,) * len(shape))
    window = jax.ShapeDtypeStruct((extent, BS, cols), jnp.bfloat16)
    return pl.pallas_call(
        forward_kernel,
        grid_spec=pltpu.PrefetchScalarGridSpec(
            num_scalar_prefetch=2,
            grid=(blocks,),
            in_specs=[
                pl.BlockSpec((BS, cols), lambda i, *_: (i, 0)),
                whole(rows, cols),
                whole(rows, cols),
                whole(rows, 2 * cols),
                whole(rows, 2 * cols),
            ],
            out_specs=[
                pl.BlockSpec((cols, BS), lambda i, *_: (0, i)),
                pl.BlockSpec((1, slots * BS, 2 * BS), lambda i, *_: (i, 0, 0)),
                whole(extent, BS, cols),
                whole(extent, BS, cols),
            ],
            scratch_shapes=[
                pltpu.VMEM((extent, BS, cols), jnp.bfloat16),
                pltpu.VMEM((extent, BS, cols), jnp.bfloat16),
                pltpu.VMEM((slots * BS, 2 * BS), jnp.float32),
            ],
        ),
        out_shape=[
            jax.ShapeDtypeStruct((cols, rows), jnp.bfloat16),
            jax.ShapeDtypeStruct((blocks, slots * BS, 2 * BS), jnp.float32),
            window,
            window,
        ],
        compiler_params=pltpu.CompilerParams(dimension_semantics=("arbitrary",)),
        cost_estimate=cost(blocks),
        name="forward",
    )(places, active, query_rows, key_rows, value_rows, left, right)


def backward_kernel(own, places, active, halo, q_ref, ga_ref, att_ref, p_ref, kt_ref, v_ref, *rest):
    if own:
        base_ref, dq_ref, dk, dv = rest
    else:
        dq_ref, left_ref, right_ref, dk, dv = rest
    step = pl.program_id(0)
    slots = p_ref.shape[1] // BS
    blocks = v_ref.shape[0] // 3
    factor = HD ** (-0.5)

    @pl.when(step == 0)
    def _():
        dk[...] = jnp.zeros_like(dk)
        dv[...] = jnp.zeros_like(dv)

    grad = ga_ref[...]
    grad_t = grad.T
    products = grad_t.astype(jnp.float32) * att_ref[...].astype(jnp.float32)
    dots = jnp.concatenate(
        [
            jnp.sum(products[:HD], axis=0, keepdims=True),
            jnp.sum(products[HD:], axis=0, keepdims=True),
        ],
        axis=1,
    )
    grad_wide = spread_columns(grad_t)
    grad_tall = spread_rows(grad)
    query_tall = spread_rows(q_ref[...] * factor)
    begin = halo[step] if own else 0
    used = active[step] - halo[step] if own else halo[step]

    def run(size):
        total = None
        for s in range(0, size, 2):
            changes, pair = [], []
            for j in range(2):
                slot = begin + s + j
                final = s + j == size - 1
                if final:
                    slot = jnp.minimum(slot, slots - 1)
                place = places[step, slot]
                rows = pl.ds(pl.multiple_of(slot * BS, BS), BS)
                weights = p_ref[0, rows, :]
                if final:
                    weights = jnp.where(s + j < used, weights, 0.0)
                change = weights * (dot(v_ref[place], grad_wide) - dots)
                change = change.astype(jnp.bfloat16)
                changes.append(change)
                pair.append(kt_ref[place])
                at = place - blocks if own else jnp.where(place < blocks, place, place - blocks)
                at = jnp.clip(at, 0, dk.shape[0] - 1)
                dk[at] += dot(change, query_tall)
                dv[at] += dot(weights.astype(jnp.bfloat16), grad_tall)
            term = dot(jnp.concatenate(pair, axis=1), jnp.concatenate(changes, axis=0))
            total = term if total is None else total + term
        total = own_heads(total)
        if own:
            dq_ref[...] = ((total + base_ref[...]) * factor).T.astype(jnp.bfloat16)
        else:
            dq_ref[...] = total

    by_size(used, run)

    if not own:

        @pl.when(step == pl.num_programs(0) - 1)
        def _():
            for b in range(2 * blocks):
                side, at = divmod(b, blocks)
                target = (left_ref, right_ref)[side]
                rows = pl.ds(at * BS, BS)
                target[rows, :BS] = dk[b].astype(target.dtype)
                target[rows, BS:] = dv[b].astype(target.dtype)


def backward(tables, query_rows, grad_attended, att_t, weights, keys_t, values, base):
    blocks, slots = tables[0].shape
    rows, cols = query_rows.shape
    extent = 3 * blocks
    own = bool(base)
    whole = lambda *shape: pl.BlockSpec(shape, lambda i, *_: (0,) * len(shape))
    one = pl.BlockSpec((BS, cols), lambda i, *_: (i, 0))
    one_t = pl.BlockSpec((cols, BS), lambda i, *_: (0, i))
    in_specs = [
        one,
        one,
        one_t,
        pl.BlockSpec((1, slots * BS, 2 * BS), lambda i, *_: (i, 0, 0)),
        whole(extent, BS, cols),
        whole(extent, BS, cols),
    ]
    if own:
        in_specs.append(one_t)
        out_specs = [one] + [whole(blocks, BS, cols)] * 2
        out_shape = [jax.ShapeDtypeStruct((rows, cols), jnp.bfloat16)]
        out_shape += [jax.ShapeDtypeStruct((blocks, BS, cols), jnp.float32)] * 2
        scratch = []
    else:
        out_specs = [one_t] + [whole(rows, 2 * cols)] * 2
        out_shape = [jax.ShapeDtypeStruct((cols, rows), jnp.float32)]
        out_shape += [jax.ShapeDtypeStruct((rows, 2 * cols), jnp.bfloat16)] * 2
        scratch = [pltpu.VMEM((2 * blocks, BS, cols), jnp.float32)] * 2
    return pl.pallas_call(
        functools.partial(backward_kernel, own),
        grid_spec=pltpu.PrefetchScalarGridSpec(
            num_scalar_prefetch=3,
            grid=(blocks,),
            in_specs=in_specs,
            out_specs=out_specs,
            scratch_shapes=scratch,
        ),
        out_shape=out_shape,
        compiler_params=pltpu.CompilerParams(dimension_semantics=("arbitrary",)),
        cost_estimate=cost(blocks),
        name="backward",
    )(*tables, query_rows, grad_attended, att_t, weights, keys_t, values, *base)


def shifted(x, axis, by):
    count = lax.axis_size(axis)
    return lax.ppermute(x, axis, [(i, (i + by) % count) for i in range(count)])


def project_kernel(g_ref, w_ref, att_ref, ga_ref, wg_ref):
    count = g_ref.shape[0]
    att = att_ref[...]
    total = None
    for k in range(0, count, 2):
        part = jnp.concatenate([g_ref[k], g_ref[k + 1]], axis=1)
        side = w_ref[:, k * BS : (k + 2) * BS]
        term = lax.dot_general(
            part, side, (((1,), (1,)), ((), ())), preferred_element_type=jnp.float32
        )
        total = term if total is None else total + term
        grad = dot(att, part)
        for j in range(2):
            wg_ref[k + j] = grad[:, j * BS : (j + 1) * BS].astype(wg_ref.dtype)
    ga_ref[...] = total.astype(jnp.bfloat16)


def project(gathered, out_weight, att_t):
    count, rows, width = gathered.shape
    cols = out_weight.shape[0]
    return pl.pallas_call(
        project_kernel,
        in_specs=[pl.BlockSpec(memory_space=pltpu.VMEM)] * 3,
        out_shape=[
            jax.ShapeDtypeStruct((rows, cols), jnp.bfloat16),
            jax.ShapeDtypeStruct((count, cols, width), jnp.bfloat16),
        ],
        cost_estimate=cost(2),
        name="project",
    )(gathered, out_weight, att_t)


def place_kernel(sum_ref, out_ref):
    for k in range(sum_ref.shape[0]):
        out_ref[:, k * BS : (k + 1) * BS] = sum_ref[k].astype(jnp.float32)


def place(sums):
    count, cols, width = sums.shape
    return pl.pallas_call(
        place_kernel,
        out_shape=jax.ShapeDtypeStruct((cols, count * width), jnp.float32),
        name="place",
    )(sums)


def gather_heads(rows):
    copies = jnp.broadcast_to(rows[None], (lax.axis_size("head"),) + rows.shape)
    return lax.all_to_all(copies, "head", 0, 0)


def slot_tables(neighbours, counts, blocks):
    first = lax.axis_index("ctx") * blocks
    places = lax.dynamic_slice_in_dim(neighbours, first, blocks, axis=0)
    places = jnp.clip(places - (first - blocks), 0, 3 * blocks - 1)
    active = lax.dynamic_slice_in_dim(counts, first, blocks, axis=0)
    slots = jnp.arange(places.shape[1], dtype=jnp.int32)
    own = (places >= blocks) & (places < 2 * blocks)
    kind = jnp.where(slots < active[:, None], own.astype(jnp.int32), 2)
    key = kind * places.shape[1] + slots
    rank = jnp.sum((key[:, :, None] > key[:, None, :]).astype(jnp.int32), axis=2)
    chosen = rank[:, :, None] == slots
    ordered = jnp.sum(jnp.where(chosen, places[:, :, None], 0), axis=1)
    halo = jnp.sum((kind == 0).astype(jnp.int32), axis=1)
    return ordered, active, halo


def body(query_rows, key_rows, value_rows, out_grad, out_weight, neighbours, counts):
    row_count, col_count = query_rows.shape
    blocks = row_count // BS
    node_count = row_count * lax.axis_size("ctx")
    gathered = gather_heads(out_grad)
    packed = jnp.concatenate([key_rows, value_rows], axis=1)
    left = shifted(packed, "ctx", 1)
    right = shifted(packed, "ctx", -1)
    tables = slot_tables(neighbours, counts, blocks)
    att_t, weights, keys_t, values = forward(
        *tables[:2], query_rows, key_rows, value_rows, left, right
    )
    grad_attended, partial = project(gathered, out_weight, att_t)
    shared = (query_rows, grad_attended, att_t, weights, keys_t, values)
    members = lax.axis_size("ctx")
    pieces = partial.reshape(members, -1, partial.shape[-1])
    pieces = lax.all_to_all(pieces, "ctx", 0, 0)
    query_part, to_left, to_right = backward(tables, *shared, ())
    from_right = shifted(to_left, "ctx", -1)
    from_left = shifted(to_right, "ctx", 1)
    piece = jnp.sum(pieces.astype(jnp.float32), axis=0) * node_count ** (-0.5)
    copies = jnp.broadcast_to(piece.astype(partial.dtype)[None], pieces.shape)
    weight_sum = lax.all_to_all(copies, "ctx", 0, 0)
    query_grad, key_own, value_own = backward(tables, *shared, (query_part,))
    weight_grad = place(weight_sum.reshape(partial.shape))
    sides = [
        own.reshape(row_count, col_count)
        + from_right[:, at : at + col_count].astype(jnp.float32)
        + from_left[:, at : at + col_count].astype(jnp.float32)
        for own, at in ((key_own, 0), (value_own, col_count))
    ]
    key_grad, value_grad = [side.astype(jnp.bfloat16) for side in sides]
    return (query_grad, key_grad, value_grad, weight_grad)


def solution(mesh):
    placed = (
        P("ctx", "head"),
        P("ctx", "head"),
        P("ctx", "head"),
        P("ctx", "head"),
        P("head", None),
        P(),
        P(),
    )
    return jax.shard_map(
        body,
        mesh=mesh,
        in_specs=placed,
        out_specs=(P("ctx", "head"), P("ctx", "head"), P("ctx", "head"), P("head", None)),
        check_vma=False,
    )
```

```python
import functools

import jax
import jax.numpy as jnp
from jax import lax
from jax.experimental import pallas as pl
from jax.experimental.pallas import tpu as pltpu
from jax.sharding import PartitionSpec as P


HD = 64
BS = 128
SIZES = (2, 4, 6, 8, 10, 12)


def by_size(active, run):
    low = -1
    for size in SIZES:
        pl.when((active > low) & (active <= size))(lambda size=size: run(size))
        low = size


def cost(steps):
    return pl.CostEstimate(flops=2 * steps * 10**9, bytes_accessed=steps * 10**6, transcendentals=0)


def spread_columns(rows_t):
    blank = jnp.zeros((HD, BS), rows_t.dtype)
    upper = jnp.concatenate([rows_t[:HD], blank], axis=1)
    lower = jnp.concatenate([blank, rows_t[HD:]], axis=1)
    return jnp.concatenate([upper, lower], axis=0)


def spread_rows(rows):
    lane = lax.broadcasted_iota(jnp.int32, rows.shape, 1)
    blank = jnp.zeros_like(rows)
    return jnp.concatenate(
        [jnp.where(lane < HD, rows, blank), jnp.where(lane >= HD, rows, blank)], axis=0
    )


def own_heads(both):
    return jnp.concatenate([both[:HD, :BS], both[HD:, BS:]], axis=0)


def dot(a, b):
    return jnp.dot(a, b, preferred_element_type=jnp.float32)


def forward_kernel(
    places, active, q_ref, mid_k, mid_v, left, right, att_ref, stat_ref, kt_ref, k_scr, vt_scr, s_scr
):
    step = pl.program_id(0)

    @pl.when(step == 0)
    def _():
        count = mid_k.shape[0] // BS
        for b in range(3 * count):
            side, at = divmod(b, count)
            rows = pl.ds(at * BS, BS)
            if side == 1:
                k, v = mid_k[rows, :], mid_v[rows, :]
            else:
                source = left if side == 0 else right
                k, v = source[rows, :BS], source[rows, BS:]
            k_scr[b] = k
            kt_ref[b] = k.T
            vt_scr[b] = v.T

    query = spread_columns(q_ref[...].T * HD ** (-0.5))

    def run(size):
        highest = None
        for s in range(size):
            scores = dot(k_scr[places[step, s]], query)
            if s == size - 1:
                scores = jnp.where(s < active[step], scores, -1e30)
            s_scr[pl.ds(s * BS, BS), :] = scores
            part = jnp.max(scores.reshape(BS // 8, 8, 2 * BS), axis=0)
            highest = part if highest is None else jnp.maximum(highest, part)
        highest = jnp.max(highest, axis=0, keepdims=True)
        total = None
        for s in range(size):
            grown = jnp.exp(s_scr[pl.ds(s * BS, BS), :] - highest)
            s_scr[pl.ds(s * BS, BS), :] = grown
            part = jnp.sum(grown.reshape(BS // 8, 8, 2 * BS), axis=0)
            total = part if total is None else total + part
        inverse = 1.0 / jnp.sum(total, axis=0, keepdims=True)
        stat_ref[0, 0:1, :] = highest
        stat_ref[0, 1:2, :] = inverse
        attended = None
        for s in range(0, size, 2):
            weights = s_scr[pl.ds(s * BS, 2 * BS), :] * inverse
            pair = jnp.concatenate([vt_scr[places[step, s]], vt_scr[places[step, s + 1]]], axis=1)
            term = dot(pair, weights.astype(jnp.bfloat16))
            attended = term if attended is None else attended + term
        att_ref[...] = own_heads(attended).astype(jnp.bfloat16)

    by_size(active[step], run)


def forward(places, active, query_rows, key_rows, value_rows, left, right):
    blocks, slots = places.shape
    rows, cols = query_rows.shape
    extent = 3 * blocks
    whole = lambda *shape: pl.BlockSpec(shape, lambda i, *_: (0,) * len(shape))
    return pl.pallas_call(
        forward_kernel,
        grid_spec=pltpu.PrefetchScalarGridSpec(
            num_scalar_prefetch=2,
            grid=(blocks,),
            in_specs=[
                pl.BlockSpec((BS, cols), lambda i, *_: (i, 0)),
                whole(rows, cols),
                whole(rows, cols),
                whole(rows, 2 * cols),
                whole(rows, 2 * cols),
            ],
            out_specs=[
                pl.BlockSpec((cols, BS), lambda i, *_: (0, i)),
                pl.BlockSpec((1, 8, 2 * BS), lambda i, *_: (i, 0, 0)),
                whole(extent, BS, cols),
            ],
            scratch_shapes=[
                pltpu.VMEM((extent, BS, cols), jnp.bfloat16),
                pltpu.VMEM((extent, BS, cols), jnp.bfloat16),
                pltpu.VMEM((slots * BS, 2 * BS), jnp.float32),
            ],
        ),
        out_shape=[
            jax.ShapeDtypeStruct((cols, rows), jnp.bfloat16),
            jax.ShapeDtypeStruct((blocks, 8, 2 * BS), jnp.float32),
            jax.ShapeDtypeStruct((extent, BS, cols), jnp.bfloat16),
        ],
        compiler_params=pltpu.CompilerParams(dimension_semantics=("arbitrary",)),
        cost_estimate=cost(blocks),
        name="forward",
    )(places, active, query_rows, key_rows, value_rows, left, right)


def backward_kernel(own, places, active, halo, q_ref, ga_ref, att_ref, stat_ref, kt_ref, first, second, *rest):
    if own:
        base_ref, dq_ref, dk, dv, k_scr, v_scr = rest
    else:
        dq_ref, left_ref, right_ref, dk, dv, k_scr, v_scr = rest
    step = pl.program_id(0)
    slots = places.shape[1]
    blocks = first.shape[0] // BS
    factor = HD ** (-0.5)

    @pl.when(step == 0)
    def _():
        dk[...] = jnp.zeros_like(dk)
        dv[...] = jnp.zeros_like(dv)
        for b in range(blocks):
            rows = pl.ds(b * BS, BS)
            if own:
                k_scr[b] = first[rows, :]
                v_scr[b] = second[rows, :]
            else:
                k_scr[b] = first[rows, :BS]
                v_scr[b] = first[rows, BS:]
                k_scr[b + blocks] = second[rows, :BS]
                v_scr[b + blocks] = second[rows, BS:]

    grad = ga_ref[...]
    grad_t = grad.T
    products = grad_t.astype(jnp.float32) * att_ref[...].astype(jnp.float32)
    dots = jnp.concatenate(
        [
            jnp.sum(products[:HD], axis=0, keepdims=True),
            jnp.sum(products[HD:], axis=0, keepdims=True),
        ],
        axis=1,
    )
    grad_wide = spread_columns(grad_t)
    grad_tall = spread_rows(grad)
    query = q_ref[...] * factor
    query_tall = spread_rows(query)
    query_wide = spread_columns(query.T)
    highest = stat_ref[0, 0:1, :]
    inverse = stat_ref[0, 1:2, :]
    begin = halo[step] if own else 0
    used = active[step] - halo[step] if own else halo[step]

    def run(size):
        total = None
        for s in range(0, size, 2):
            changes, pair = [], []
            for j in range(2):
                slot = begin + s + j
                final = s + j == size - 1
                if final:
                    slot = jnp.minimum(slot, slots - 1)
                place = places[step, slot]
                at = place - blocks if own else jnp.where(place < blocks, place, place - blocks)
                at = jnp.clip(at, 0, dk.shape[0] - 1)
                weights = jnp.exp(dot(k_scr[at], query_wide) - highest) * inverse
                if final:
                    weights = jnp.where(s + j < used, weights, 0.0)
                change = weights * (dot(v_scr[at], grad_wide) - dots)
                change = change.astype(jnp.bfloat16)
                changes.append(change)
                pair.append(kt_ref[at] if own else kt_ref[place])
                dk[at] += dot(change, query_tall)
                dv[at] += dot(weights.astype(jnp.bfloat16), grad_tall)
            term = dot(jnp.concatenate(pair, axis=1), jnp.concatenate(changes, axis=0))
            total = term if total is None else total + term
        total = own_heads(total)
        if own:
            dq_ref[...] = ((total + base_ref[...]) * factor).T.astype(jnp.bfloat16)
        else:
            dq_ref[...] = total

    by_size(used, run)

    if not own:

        @pl.when(step == pl.num_programs(0) - 1)
        def _():
            for b in range(2 * blocks):
                side, at = divmod(b, blocks)
                target = (left_ref, right_ref)[side]
                rows = pl.ds(at * BS, BS)
                target[rows, :BS] = dk[b].astype(target.dtype)
                target[rows, BS:] = dv[b].astype(target.dtype)


def backward(tables, query_rows, grad_attended, att_t, stats, keys_t, sources, base):
    blocks, _ = tables[0].shape
    rows, cols = query_rows.shape
    extent = 3 * blocks
    own = bool(base)
    held = blocks if own else 2 * blocks
    whole = lambda *shape: pl.BlockSpec(shape, lambda i, *_: (0,) * len(shape))
    one = pl.BlockSpec((BS, cols), lambda i, *_: (i, 0))
    one_t = pl.BlockSpec((cols, BS), lambda i, *_: (0, i))
    in_specs = [
        one,
        one,
        one_t,
        pl.BlockSpec((1, 8, 2 * BS), lambda i, *_: (i, 0, 0)),
        pl.BlockSpec((blocks, BS, cols), lambda i, *_: (1, 0, 0)) if own else whole(extent, BS, cols),
        whole(*sources[0].shape),
        whole(*sources[1].shape),
    ]
    scratch = []
    if own:
        in_specs.append(one_t)
        out_specs = [one] + [whole(blocks, BS, cols)] * 2
        out_shape = [jax.ShapeDtypeStruct((rows, cols), jnp.bfloat16)]
        out_shape += [jax.ShapeDtypeStruct((blocks, BS, cols), jnp.float32)] * 2
    else:
        out_specs = [one_t] + [whole(rows, 2 * cols)] * 2
        out_shape = [jax.ShapeDtypeStruct((cols, rows), jnp.float32)]
        out_shape += [jax.ShapeDtypeStruct((rows, 2 * cols), jnp.bfloat16)] * 2
        scratch = [pltpu.VMEM((held, BS, cols), jnp.float32)] * 2
    scratch += [pltpu.VMEM((held, BS, cols), jnp.bfloat16)] * 2
    return pl.pallas_call(
        functools.partial(backward_kernel, own),
        grid_spec=pltpu.PrefetchScalarGridSpec(
            num_scalar_prefetch=3,
            grid=(blocks,),
            in_specs=in_specs,
            out_specs=out_specs,
            scratch_shapes=scratch,
        ),
        out_shape=out_shape,
        compiler_params=pltpu.CompilerParams(dimension_semantics=("arbitrary",)),
        cost_estimate=cost(blocks),
        name="backward",
    )(*tables, query_rows, grad_attended, att_t, stats, keys_t, *sources, *base)


def shifted(x, axis, by):
    count = lax.axis_size(axis)
    return lax.ppermute(x, axis, [(i, (i + by) % count) for i in range(count)])


def project_kernel(g_ref, w_ref, att_ref, ga_ref, wg_ref):
    count = g_ref.shape[0]
    att = att_ref[...]
    total = None
    for k in range(0, count, 2):
        part = jnp.concatenate([g_ref[k], g_ref[k + 1]], axis=1)
        side = w_ref[:, k * BS : (k + 2) * BS]
        term = lax.dot_general(
            part, side, (((1,), (1,)), ((), ())), preferred_element_type=jnp.float32
        )
        total = term if total is None else total + term
        grad = dot(att, part)
        for j in range(2):
            wg_ref[k + j] = grad[:, j * BS : (j + 1) * BS].astype(wg_ref.dtype)
    ga_ref[...] = total.astype(jnp.bfloat16)


def project(gathered, out_weight, att_t):
    count, rows, width = gathered.shape
    cols = out_weight.shape[0]
    return pl.pallas_call(
        project_kernel,
        in_specs=[pl.BlockSpec(memory_space=pltpu.VMEM)] * 3,
        out_shape=[
            jax.ShapeDtypeStruct((rows, cols), jnp.bfloat16),
            jax.ShapeDtypeStruct((count, cols, width), jnp.bfloat16),
        ],
        cost_estimate=cost(2),
        name="project",
    )(gathered, out_weight, att_t)


def place_kernel(sum_ref, out_ref):
    for k in range(sum_ref.shape[0]):
        out_ref[:, k * BS : (k + 1) * BS] = sum_ref[k].astype(jnp.float32)


def place(sums):
    count, cols, width = sums.shape
    return pl.pallas_call(
        place_kernel,
        out_shape=jax.ShapeDtypeStruct((cols, count * width), jnp.float32),
        name="place",
    )(sums)


def gather_heads(rows):
    copies = jnp.broadcast_to(rows[None], (lax.axis_size("head"),) + rows.shape)
    return lax.all_to_all(copies, "head", 0, 0)


def slot_tables(neighbours, counts, blocks):
    first = lax.axis_index("ctx") * blocks
    places = lax.dynamic_slice_in_dim(neighbours, first, blocks, axis=0)
    places = jnp.clip(places - (first - blocks), 0, 3 * blocks - 1)
    active = lax.dynamic_slice_in_dim(counts, first, blocks, axis=0)
    slots = jnp.arange(places.shape[1], dtype=jnp.int32)
    own = (places >= blocks) & (places < 2 * blocks)
    kind = jnp.where(slots < active[:, None], own.astype(jnp.int32), 2)
    key = kind * places.shape[1] + slots
    rank = jnp.sum((key[:, :, None] > key[:, None, :]).astype(jnp.int32), axis=2)
    chosen = rank[:, :, None] == slots
    ordered = jnp.sum(jnp.where(chosen, places[:, :, None], 0), axis=1)
    halo = jnp.sum((kind == 0).astype(jnp.int32), axis=1)
    return ordered, active, halo


def body(query_rows, key_rows, value_rows, out_grad, out_weight, neighbours, counts):
    row_count, col_count = query_rows.shape
    blocks = row_count // BS
    node_count = row_count * lax.axis_size("ctx")
    gathered = gather_heads(out_grad)
    packed = jnp.concatenate([key_rows, value_rows], axis=1)
    left = shifted(packed, "ctx", 1)
    right = shifted(packed, "ctx", -1)
    tables = slot_tables(neighbours, counts, blocks)
    att_t, stats, keys_t = forward(
        *tables[:2], query_rows, key_rows, value_rows, left, right
    )
    grad_attended, partial = project(gathered, out_weight, att_t)
    shared = (query_rows, grad_attended, att_t, stats, keys_t)
    members = lax.axis_size("ctx")
    pieces = partial.reshape(members, -1, partial.shape[-1])
    pieces = lax.all_to_all(pieces, "ctx", 0, 0)
    query_part, to_left, to_right = backward(tables, *shared, (left, right), ())
    from_right = shifted(to_left, "ctx", -1)
    from_left = shifted(to_right, "ctx", 1)
    piece = jnp.sum(pieces.astype(jnp.float32), axis=0) * node_count ** (-0.5)
    copies = jnp.broadcast_to(piece.astype(partial.dtype)[None], pieces.shape)
    weight_sum = lax.all_to_all(copies, "ctx", 0, 0)
    query_grad, key_own, value_own = backward(
        tables, *shared, (key_rows, value_rows), (query_part,)
    )
    weight_grad = place(weight_sum.reshape(partial.shape))
    sides = [
        own.reshape(row_count, col_count)
        + from_right[:, at : at + col_count].astype(jnp.float32)
        + from_left[:, at : at + col_count].astype(jnp.float32)
        for own, at in ((key_own, 0), (value_own, col_count))
    ]
    key_grad, value_grad = [side.astype(jnp.bfloat16) for side in sides]
    return (query_grad, key_grad, value_grad, weight_grad)


def solution(mesh):
    placed = (
        P("ctx", "head"),
        P("ctx", "head"),
        P("ctx", "head"),
        P("ctx", "head"),
        P("head", None),
        P(),
        P(),
    )
    return jax.shard_map(
        body,
        mesh=mesh,
        in_specs=placed,
        out_specs=(P("ctx", "head"), P("ctx", "head"), P("ctx", "head"), P("head", None)),
        check_vma=False,
    )
```

```python
import functools

import jax
import jax.numpy as jnp
from jax import lax
from jax.experimental import pallas as pl
from jax.experimental.pallas import tpu as pltpu
from jax.sharding import PartitionSpec as P


HD = 64
BS = 128
SIZES = (2, 4, 6, 8, 10, 12)


def by_size(active, run):
    low = -1
    for size in SIZES:
        pl.when((active > low) & (active <= size))(lambda size=size: run(size))
        low = size


def cost(steps):
    return pl.CostEstimate(flops=2 * steps * 10**9, bytes_accessed=steps * 10**6, transcendentals=0)


def spread_columns(rows_t):
    blank = jnp.zeros((HD, BS), rows_t.dtype)
    upper = jnp.concatenate([rows_t[:HD], blank], axis=1)
    lower = jnp.concatenate([blank, rows_t[HD:]], axis=1)
    return jnp.concatenate([upper, lower], axis=0)


def spread_rows(rows):
    lane = lax.broadcasted_iota(jnp.int32, rows.shape, 1)
    blank = jnp.zeros_like(rows)
    return jnp.concatenate(
        [jnp.where(lane < HD, rows, blank), jnp.where(lane >= HD, rows, blank)], axis=0
    )


def own_heads(both):
    return jnp.concatenate([both[:HD, :BS], both[HD:, BS:]], axis=0)


def dot(a, b):
    return jnp.dot(a, b, preferred_element_type=jnp.float32)


def forward_kernel(
    places, active, q_ref, mid_k, mid_v, left, right, att_ref, stat_ref, kt_ref, k_scr, vt_scr, s_scr
):
    step = pl.program_id(0)

    @pl.when(step == 0)
    def _():
        count = mid_k.shape[0] // BS
        for b in range(3 * count):
            side, at = divmod(b, count)
            rows = pl.ds(at * BS, BS)
            if side == 1:
                k, v = mid_k[rows, :], mid_v[rows, :]
            else:
                source = left if side == 0 else right
                k, v = source[rows, :BS], source[rows, BS:]
            k_scr[b] = k
            kt_ref[b] = k.T
            vt_scr[b] = v.T

    query = spread_columns(q_ref[...].T * HD ** (-0.5))

    def run(size):
        highest = None
        for s in range(size):
            scores = dot(k_scr[places[step, s]], query)
            if s == size - 1:
                scores = jnp.where(s < active[step], scores, -1e30)
            s_scr[pl.ds(s * BS, BS), :] = scores
            part = jnp.max(scores.reshape(BS // 8, 8, 2 * BS), axis=0)
            highest = part if highest is None else jnp.maximum(highest, part)
        highest = jnp.max(highest, axis=0, keepdims=True)
        total = None
        for s in range(size):
            grown = jnp.exp(s_scr[pl.ds(s * BS, BS), :] - highest)
            s_scr[pl.ds(s * BS, BS), :] = grown
            part = jnp.sum(grown.reshape(BS // 8, 8, 2 * BS), axis=0)
            total = part if total is None else total + part
        inverse = 1.0 / jnp.sum(total, axis=0, keepdims=True)
        stat_ref[0, 0:1, :] = highest
        stat_ref[0, 1:2, :] = inverse
        attended = None
        for s in range(0, size, 2):
            weights = s_scr[pl.ds(s * BS, 2 * BS), :] * inverse
            pair = jnp.concatenate([vt_scr[places[step, s]], vt_scr[places[step, s + 1]]], axis=1)
            term = dot(pair, weights.astype(jnp.bfloat16))
            attended = term if attended is None else attended + term
        att_ref[...] = own_heads(attended).astype(jnp.bfloat16)

    by_size(active[step], run)


def forward(places, active, query_rows, key_rows, value_rows, left, right):
    blocks, slots = places.shape
    rows, cols = query_rows.shape
    extent = 3 * blocks
    whole = lambda *shape: pl.BlockSpec(shape, lambda i, *_: (0,) * len(shape))
    return pl.pallas_call(
        forward_kernel,
        grid_spec=pltpu.PrefetchScalarGridSpec(
            num_scalar_prefetch=2,
            grid=(blocks,),
            in_specs=[
                pl.BlockSpec((BS, cols), lambda i, *_: (i, 0)),
                whole(rows, cols),
                whole(rows, cols),
                whole(rows, 2 * cols),
                whole(rows, 2 * cols),
            ],
            out_specs=[
                pl.BlockSpec((cols, BS), lambda i, *_: (0, i)),
                pl.BlockSpec((1, 8, 2 * BS), lambda i, *_: (i, 0, 0)),
                whole(extent, BS, cols),
            ],
            scratch_shapes=[
                pltpu.VMEM((extent, BS, cols), jnp.bfloat16),
                pltpu.VMEM((extent, BS, cols), jnp.bfloat16),
                pltpu.VMEM((slots * BS, 2 * BS), jnp.float32),
            ],
        ),
        out_shape=[
            jax.ShapeDtypeStruct((cols, rows), jnp.bfloat16),
            jax.ShapeDtypeStruct((blocks, 8, 2 * BS), jnp.float32),
            jax.ShapeDtypeStruct((extent, BS, cols), jnp.bfloat16),
        ],
        compiler_params=pltpu.CompilerParams(dimension_semantics=("arbitrary",)),
        cost_estimate=cost(blocks),
        name="forward",
    )(places, active, query_rows, key_rows, value_rows, left, right)


def backward_kernel(own, places, active, halo, q_ref, ga_ref, att_ref, stat_ref, kt_ref, first, second, *rest):
    gw_scr, gt_scr, qw_scr, qt_scr, dot_scr = rest[-5:]
    if own:
        base_ref, dq_ref, dk, dv, k_scr, v_scr, dq_scr = rest[:-5]
    else:
        dq_ref, left_ref, right_ref, dk, dv, k_scr, v_scr = rest[:-5]
    step = pl.program_id(0)
    slots = places.shape[1]
    blocks = first.shape[0] // BS
    factor = HD ** (-0.5)

    @pl.when(step == 0)
    def _():
        dk[...] = jnp.zeros_like(dk)
        dv[...] = jnp.zeros_like(dv)
        for b in range(blocks):
            rows = pl.ds(b * BS, BS)
            grad = ga_ref[rows, :]
            grad_t = grad.T
            products = grad_t.astype(jnp.float32) * att_ref[:, rows].astype(jnp.float32)
            dot_scr[b, 0:1, :BS] = jnp.sum(products[:HD], axis=0, keepdims=True)
            dot_scr[b, 0:1, BS:] = jnp.sum(products[HD:], axis=0, keepdims=True)
            gw_scr[b] = spread_columns(grad_t)
            gt_scr[b] = spread_rows(grad)
            query = q_ref[rows, :] * factor
            qw_scr[b] = spread_columns(query.T)
            qt_scr[b] = spread_rows(query)
            if own:
                k_scr[b] = first[rows, :]
                v_scr[b] = second[rows, :]
            else:
                k_scr[b] = first[rows, :BS]
                v_scr[b] = first[rows, BS:]
                k_scr[b + blocks] = second[rows, :BS]
                v_scr[b + blocks] = second[rows, BS:]

    grad_wide, grad_tall = gw_scr[step], gt_scr[step]
    query_wide, query_tall = qw_scr[step], qt_scr[step]
    dots = dot_scr[step, 0:1, :]
    highest = stat_ref[step, 0:1, :]
    inverse = stat_ref[step, 1:2, :]
    begin = halo[step] if own else 0
    used = active[step] - halo[step] if own else halo[step]

    def run(size):
        total = None
        for s in range(0, size, 2):
            changes, pair = [], []
            for j in range(2):
                slot = begin + s + j
                final = s + j == size - 1
                if final:
                    slot = jnp.minimum(slot, slots - 1)
                place = places[step, slot]
                at = place - blocks if own else jnp.where(place < blocks, place, place - blocks)
                at = jnp.clip(at, 0, dk.shape[0] - 1)
                weights = jnp.exp(dot(k_scr[at], query_wide) - highest) * inverse
                if final:
                    weights = jnp.where(s + j < used, weights, 0.0)
                change = weights * (dot(v_scr[at], grad_wide) - dots)
                change = change.astype(jnp.bfloat16)
                changes.append(change)
                pair.append(kt_ref[at] if own else kt_ref[place])
                dk[at] += dot(change, query_tall)
                dv[at] += dot(weights.astype(jnp.bfloat16), grad_tall)
            term = dot(jnp.concatenate(pair, axis=1), jnp.concatenate(changes, axis=0))
            total = term if total is None else total + term
        total = own_heads(total)
        if own:
            dq_scr[step] = (total + base_ref[...]) * factor
        else:
            dq_ref[...] = total

    by_size(used, run)

    @pl.when(step == pl.num_programs(0) - 1)
    def _():
        if own:
            for b in range(blocks):
                dq_ref[pl.ds(b * BS, BS), :] = dq_scr[b].T.astype(jnp.bfloat16)
        else:
            for b in range(2 * blocks):
                side, at = divmod(b, blocks)
                target = (left_ref, right_ref)[side]
                rows = pl.ds(at * BS, BS)
                target[rows, :BS] = dk[b].astype(target.dtype)
                target[rows, BS:] = dv[b].astype(target.dtype)


def backward(tables, query_rows, grad_attended, att_t, stats, keys_t, sources, base):
    blocks, _ = tables[0].shape
    rows, cols = query_rows.shape
    extent = 3 * blocks
    own = bool(base)
    held = blocks if own else 2 * blocks
    whole = lambda *shape: pl.BlockSpec(shape, lambda i, *_: (0,) * len(shape))
    one_t = pl.BlockSpec((cols, BS), lambda i, *_: (0, i))
    in_specs = [
        whole(rows, cols),
        whole(rows, cols),
        whole(cols, rows),
        whole(*stats.shape),
        pl.BlockSpec((blocks, BS, cols), lambda i, *_: (1, 0, 0)) if own else whole(extent, BS, cols),
        whole(*sources[0].shape),
        whole(*sources[1].shape),
    ]
    scratch = []
    if own:
        in_specs.append(one_t)
        out_specs = [whole(rows, cols)] + [whole(blocks, BS, cols)] * 2
        out_shape = [jax.ShapeDtypeStruct((rows, cols), jnp.bfloat16)]
        out_shape += [jax.ShapeDtypeStruct((blocks, BS, cols), jnp.float32)] * 2
    else:
        out_specs = [one_t] + [whole(rows, 2 * cols)] * 2
        out_shape = [jax.ShapeDtypeStruct((cols, rows), jnp.float32)]
        out_shape += [jax.ShapeDtypeStruct((rows, 2 * cols), jnp.bfloat16)] * 2
        scratch = [pltpu.VMEM((held, BS, cols), jnp.float32)] * 2
    scratch += [pltpu.VMEM((held, BS, cols), jnp.bfloat16)] * 2
    if own:
        scratch.append(pltpu.VMEM((blocks, cols, BS), jnp.float32))
    wide = pltpu.VMEM((blocks, cols, 2 * BS), jnp.bfloat16)
    tall = pltpu.VMEM((blocks, 2 * BS, cols), jnp.bfloat16)
    scratch += [wide, tall, wide, tall, pltpu.VMEM((blocks, 8, 2 * BS), jnp.float32)]
    return pl.pallas_call(
        functools.partial(backward_kernel, own),
        grid_spec=pltpu.PrefetchScalarGridSpec(
            num_scalar_prefetch=3,
            grid=(blocks,),
            in_specs=in_specs,
            out_specs=out_specs,
            scratch_shapes=scratch,
        ),
        out_shape=out_shape,
        compiler_params=pltpu.CompilerParams(dimension_semantics=("arbitrary",)),
        cost_estimate=cost(blocks),
        name="backward",
    )(*tables, query_rows, grad_attended, att_t, stats, keys_t, *sources, *base)


def shifted(x, axis, by):
    count = lax.axis_size(axis)
    return lax.ppermute(x, axis, [(i, (i + by) % count) for i in range(count)])


def project_kernel(g_ref, w_ref, att_ref, ga_ref, wg_ref, sums):
    step = pl.program_id(0)
    count = g_ref.shape[0]
    att = att_ref[...]
    total = None
    for k in range(0, count, 2):
        part = jnp.concatenate([g_ref[k], g_ref[k + 1]], axis=1)
        side = w_ref[:, k * BS : (k + 2) * BS]
        term = lax.dot_general(
            part, side, (((1,), (1,)), ((), ())), preferred_element_type=jnp.float32
        )
        total = term if total is None else total + term
        grad = dot(att, part)

        @pl.when(step == 0)
        def _():
            sums[k // 2] = grad

        @pl.when(step > 0)
        def _():
            sums[k // 2] += grad

    ga_ref[...] = total.astype(jnp.bfloat16)

    @pl.when(step == pl.num_programs(0) - 1)
    def _():
        for k in range(count):
            at = (k % 2) * BS
            wg_ref[k] = sums[k // 2, :, at : at + BS].astype(wg_ref.dtype)


def project(gathered, out_weight, att_t):
    count, rows, width = gathered.shape
    cols = out_weight.shape[0]
    steps = 4
    each = rows // steps
    return pl.pallas_call(
        project_kernel,
        grid=(steps,),
        in_specs=[
            pl.BlockSpec((count, each, width), lambda i: (0, i, 0)),
            pl.BlockSpec((cols, count * width), lambda i: (0, 0)),
            pl.BlockSpec((cols, each), lambda i: (0, i)),
        ],
        out_specs=[
            pl.BlockSpec((each, cols), lambda i: (i, 0)),
            pl.BlockSpec((count, cols, width), lambda i: (0, 0, 0)),
        ],
        out_shape=[
            jax.ShapeDtypeStruct((rows, cols), jnp.bfloat16),
            jax.ShapeDtypeStruct((count, cols, width), jnp.bfloat16),
        ],
        scratch_shapes=[pltpu.VMEM((count // 2, cols, 2 * width), jnp.float32)],
        compiler_params=pltpu.CompilerParams(dimension_semantics=("arbitrary",)),
        cost_estimate=cost(2),
        name="project",
    )(gathered, out_weight, att_t)


def place_kernel(sum_ref, out_ref):
    for k in range(sum_ref.shape[0]):
        out_ref[:, k * BS : (k + 1) * BS] = sum_ref[k].astype(jnp.float32)


def place(sums):
    count, cols, width = sums.shape
    return pl.pallas_call(
        place_kernel,
        out_shape=jax.ShapeDtypeStruct((cols, count * width), jnp.float32),
        name="place",
    )(sums)


def gather_heads(rows):
    copies = jnp.broadcast_to(rows[None], (lax.axis_size("head"),) + rows.shape)
    return lax.all_to_all(copies, "head", 0, 0)


def slot_tables(neighbours, counts, blocks):
    first = lax.axis_index("ctx") * blocks
    places = lax.dynamic_slice_in_dim(neighbours, first, blocks, axis=0)
    places = jnp.clip(places - (first - blocks), 0, 3 * blocks - 1)
    active = lax.dynamic_slice_in_dim(counts, first, blocks, axis=0)
    slots = jnp.arange(places.shape[1], dtype=jnp.int32)
    own = (places >= blocks) & (places < 2 * blocks)
    kind = jnp.where(slots < active[:, None], own.astype(jnp.int32), 2)
    key = kind * places.shape[1] + slots
    rank = jnp.sum((key[:, :, None] > key[:, None, :]).astype(jnp.int32), axis=2)
    chosen = rank[:, :, None] == slots
    ordered = jnp.sum(jnp.where(chosen, places[:, :, None], 0), axis=1)
    halo = jnp.sum((kind == 0).astype(jnp.int32), axis=1)
    return ordered, active, halo


def body(query_rows, key_rows, value_rows, out_grad, out_weight, neighbours, counts):
    row_count, col_count = query_rows.shape
    blocks = row_count // BS
    node_count = row_count * lax.axis_size("ctx")
    gathered = gather_heads(out_grad)
    packed = jnp.concatenate([key_rows, value_rows], axis=1)
    left = shifted(packed, "ctx", 1)
    right = shifted(packed, "ctx", -1)
    tables = slot_tables(neighbours, counts, blocks)
    att_t, stats, keys_t = forward(
        *tables[:2], query_rows, key_rows, value_rows, left, right
    )
    grad_attended, partial = project(gathered, out_weight, att_t)
    shared = (query_rows, grad_attended, att_t, stats, keys_t)
    members = lax.axis_size("ctx")
    pieces = partial.reshape(members, -1, partial.shape[-1])
    pieces = lax.all_to_all(pieces, "ctx", 0, 0)
    query_part, to_left, to_right = backward(tables, *shared, (left, right), ())
    from_right = shifted(to_left, "ctx", -1)
    from_left = shifted(to_right, "ctx", 1)
    piece = jnp.sum(pieces.astype(jnp.float32), axis=0) * node_count ** (-0.5)
    copies = jnp.broadcast_to(piece.astype(partial.dtype)[None], pieces.shape)
    weight_sum = lax.all_to_all(copies, "ctx", 0, 0)
    query_grad, key_own, value_own = backward(
        tables, *shared, (key_rows, value_rows), (query_part,)
    )
    weight_grad = place(weight_sum.reshape(partial.shape))
    sides = [
        own.reshape(row_count, col_count)
        + from_right[:, at : at + col_count].astype(jnp.float32)
        + from_left[:, at : at + col_count].astype(jnp.float32)
        for own, at in ((key_own, 0), (value_own, col_count))
    ]
    key_grad, value_grad = [side.astype(jnp.bfloat16) for side in sides]
    return (query_grad, key_grad, value_grad, weight_grad)


def solution(mesh):
    placed = (
        P("ctx", "head"),
        P("ctx", "head"),
        P("ctx", "head"),
        P("ctx", "head"),
        P("head", None),
        P(),
        P(),
    )
    return jax.shard_map(
        body,
        mesh=mesh,
        in_specs=placed,
        out_specs=(P("ctx", "head"), P("ctx", "head"), P("ctx", "head"), P("head", None)),
        check_vma=False,
    )
```

```python
import functools

import jax
import jax.numpy as jnp
from jax import lax
from jax.experimental import pallas as pl
from jax.experimental.pallas import tpu as pltpu
from jax.sharding import PartitionSpec as P


HD = 64
BS = 128
SIZES = (4, 6, 8, 10, 12)
TWO = 2


def by_size(active, run, sizes=SIZES):
    low = -1
    for size in sizes:
        pl.when((active > low) & (active <= size))(lambda size=size: run(size))
        low = size


def cost(steps):
    return pl.CostEstimate(flops=2 * steps * 10**9, bytes_accessed=steps * 10**6, transcendentals=0)


def spread_columns(rows_t):
    blank = jnp.zeros((HD, BS), rows_t.dtype)
    upper = jnp.concatenate([rows_t[:HD], blank], axis=1)
    lower = jnp.concatenate([blank, rows_t[HD:]], axis=1)
    return jnp.concatenate([upper, lower], axis=0)


def spread_rows(rows):
    lane = lax.broadcasted_iota(jnp.int32, rows.shape, 1)
    blank = jnp.zeros_like(rows)
    return jnp.concatenate(
        [jnp.where(lane < HD, rows, blank), jnp.where(lane >= HD, rows, blank)], axis=0
    )


def own_heads(both):
    return jnp.concatenate([both[:HD, :BS], both[HD:, BS:]], axis=0)


def dot(a, b):
    return jnp.dot(a, b, preferred_element_type=jnp.float32)


def forward_kernel(
    places, active, q_ref, mid_k, mid_v, left, right, att_ref, stat_ref, kt_ref, k_scr, vt_scr, s_scr
):
    step = pl.program_id(0)

    @pl.when(step == 0)
    def _():
        count = mid_k.shape[0] // BS
        for b in range(3 * count):
            side, at = divmod(b, count)
            rows = pl.ds(at * BS, BS)
            if side == 1:
                k, v = mid_k[rows, :], mid_v[rows, :]
            else:
                source = left if side == 0 else right
                k, v = source[rows, :BS], source[rows, BS:]
            k_scr[b] = k
            kt_ref[b] = k.T
            vt_scr[b] = v.T

    query = spread_columns(q_ref[...].T * HD ** (-0.5))

    def run(size):
        highest = None
        for s in range(size):
            scores = dot(k_scr[places[step, s]], query)
            if s == size - 1:
                scores = jnp.where(s < active[step], scores, -1e30)
            s_scr[pl.ds(s * BS, BS), :] = scores
            part = jnp.max(scores.reshape(BS // 8, 8, 2 * BS), axis=0)
            highest = part if highest is None else jnp.maximum(highest, part)
        highest = jnp.max(highest, axis=0, keepdims=True)
        total = None
        for s in range(size):
            grown = jnp.exp(s_scr[pl.ds(s * BS, BS), :] - highest)
            s_scr[pl.ds(s * BS, BS), :] = grown
            part = jnp.sum(grown.reshape(BS // 8, 8, 2 * BS), axis=0)
            total = part if total is None else total + part
        inverse = 1.0 / jnp.sum(total, axis=0, keepdims=True)
        stat_ref[0, 0:1, :] = highest
        stat_ref[0, 1:2, :] = inverse
        attended = None
        for s in range(0, size, 2):
            weights = s_scr[pl.ds(s * BS, 2 * BS), :] * inverse
            pair = jnp.concatenate([vt_scr[places[step, s]], vt_scr[places[step, s + 1]]], axis=1)
            term = dot(pair, weights.astype(jnp.bfloat16))
            attended = term if attended is None else attended + term
        att_ref[...] = own_heads(attended).astype(jnp.bfloat16)

    by_size(active[step], run)


def forward(places, active, query_rows, key_rows, value_rows, left, right):
    blocks, slots = places.shape
    rows, cols = query_rows.shape
    extent = 3 * blocks
    whole = lambda *shape: pl.BlockSpec(shape, lambda i, *_: (0,) * len(shape))
    return pl.pallas_call(
        forward_kernel,
        grid_spec=pltpu.PrefetchScalarGridSpec(
            num_scalar_prefetch=2,
            grid=(blocks,),
            in_specs=[
                pl.BlockSpec((BS, cols), lambda i, *_: (i, 0)),
                whole(rows, cols),
                whole(rows, cols),
                whole(rows, 2 * cols),
                whole(rows, 2 * cols),
            ],
            out_specs=[
                pl.BlockSpec((cols, BS), lambda i, *_: (0, i)),
                pl.BlockSpec((1, 8, 2 * BS), lambda i, *_: (i, 0, 0)),
                whole(extent, BS, cols),
            ],
            scratch_shapes=[
                pltpu.VMEM((extent, BS, cols), jnp.bfloat16),
                pltpu.VMEM((extent, BS, cols), jnp.bfloat16),
                pltpu.VMEM((slots * BS, 2 * BS), jnp.float32),
            ],
        ),
        out_shape=[
            jax.ShapeDtypeStruct((cols, rows), jnp.bfloat16),
            jax.ShapeDtypeStruct((blocks, 8, 2 * BS), jnp.float32),
            jax.ShapeDtypeStruct((extent, BS, cols), jnp.bfloat16),
        ],
        compiler_params=pltpu.CompilerParams(dimension_semantics=("arbitrary",)),
        cost_estimate=cost(blocks),
        name="forward",
    )(places, active, query_rows, key_rows, value_rows, left, right)


def backward_kernel(own, places, active, halo, q_ref, ga_ref, att_ref, stat_ref, kt_ref, first, second, *rest):
    if own:
        base_ref, dq_ref, dk, dv, k_scr, v_scr = rest
    else:
        dq_ref, left_ref, right_ref, dk, dv, k_scr, v_scr = rest
    here = pl.program_id(0)
    slots = places.shape[1]
    blocks = first.shape[0] // BS
    factor = HD ** (-0.5)

    @pl.when(here == 0)
    def _():
        dk[...] = jnp.zeros_like(dk)
        dv[...] = jnp.zeros_like(dv)
        for b in range(blocks):
            rows = pl.ds(b * BS, BS)
            if own:
                k_scr[b] = first[rows, :]
                v_scr[b] = second[rows, :]
            else:
                k_scr[b] = first[rows, :BS]
                v_scr[b] = first[rows, BS:]
                k_scr[b + blocks] = second[rows, :BS]
                v_scr[b + blocks] = second[rows, BS:]

    held = []
    for i in range(TWO):
        step = here * TWO + i
        rows = slice(i * BS, (i + 1) * BS)
        grad = ga_ref[rows, :]
        grad_t = grad.T
        products = grad_t.astype(jnp.float32) * att_ref[:, rows].astype(jnp.float32)
        dots = jnp.concatenate(
            [
                jnp.sum(products[:HD], axis=0, keepdims=True),
                jnp.sum(products[HD:], axis=0, keepdims=True),
            ],
            axis=1,
        )
        query = q_ref[rows, :] * factor
        wide = (spread_columns(query.T), spread_columns(grad_t))
        tall = (spread_rows(query), spread_rows(grad))
        begin = halo[step] if own else 0
        used = active[step] - halo[step] if own else halo[step]
        held.append((step, rows, dots, wide, tall, begin, used))

    def run(size):
        totals = [None] * TWO
        for s in range(0, size, 2):
            for i in range(TWO):
                step, rows, dots, wide, tall, begin, used = held[i]
                changes, pair = [], []
                for j in range(2):
                    place = places[step, jnp.minimum(begin + s + j, slots - 1)]
                    at = place - blocks if own else jnp.where(place < blocks, place, place - blocks)
                    at = jnp.clip(at, 0, dk.shape[0] - 1)
                    scores = dot(k_scr[at], wide[0])
                    weights = jnp.exp(scores - stat_ref[i, 0:1, :]) * stat_ref[i, 1:2, :]
                    weights = jnp.where(s + j < used, weights, 0.0)
                    change = weights * (dot(v_scr[at], wide[1]) - dots)
                    change = change.astype(jnp.bfloat16)
                    changes.append(change)
                    pair.append(kt_ref[at] if own else kt_ref[place])
                    dk[at] += dot(change, tall[0])
                    dv[at] += dot(weights.astype(jnp.bfloat16), tall[1])
                term = dot(jnp.concatenate(pair, axis=1), jnp.concatenate(changes, axis=0))
                totals[i] = term if totals[i] is None else totals[i] + term
        for i in range(TWO):
            rows = held[i][1]
            total = own_heads(totals[i])
            if own:
                total = (total + base_ref[:, rows]) * factor
                dq_ref[rows, :] = total.T.astype(jnp.bfloat16)
            else:
                dq_ref[:, rows] = total

    by_size(jnp.maximum(held[0][-1], held[1][-1]), run, (2, 4, 6, 8, 12))

    if not own:

        @pl.when(here == pl.num_programs(0) - 1)
        def _():
            for b in range(2 * blocks):
                side, at = divmod(b, blocks)
                target = (left_ref, right_ref)[side]
                rows = pl.ds(at * BS, BS)
                target[rows, :BS] = dk[b].astype(target.dtype)
                target[rows, BS:] = dv[b].astype(target.dtype)


def backward(tables, query_rows, grad_attended, att_t, stats, keys_t, sources, base):
    blocks, _ = tables[0].shape
    rows, cols = query_rows.shape
    extent = 3 * blocks
    own = bool(base)
    held = blocks if own else 2 * blocks
    whole = lambda *shape: pl.BlockSpec(shape, lambda i, *_: (0,) * len(shape))
    one = pl.BlockSpec((TWO * BS, cols), lambda i, *_: (i, 0))
    one_t = pl.BlockSpec((cols, TWO * BS), lambda i, *_: (0, i))
    in_specs = [
        one,
        one,
        one_t,
        pl.BlockSpec((TWO, 8, 2 * BS), lambda i, *_: (i, 0, 0)),
        pl.BlockSpec((blocks, BS, cols), lambda i, *_: (1, 0, 0)) if own else whole(extent, BS, cols),
        whole(*sources[0].shape),
        whole(*sources[1].shape),
    ]
    scratch = []
    if own:
        in_specs.append(one_t)
        out_specs = [one] + [whole(blocks, BS, cols)] * 2
        out_shape = [jax.ShapeDtypeStruct((rows, cols), jnp.bfloat16)]
        out_shape += [jax.ShapeDtypeStruct((blocks, BS, cols), jnp.float32)] * 2
    else:
        out_specs = [one_t] + [whole(rows, 2 * cols)] * 2
        out_shape = [jax.ShapeDtypeStruct((cols, rows), jnp.float32)]
        out_shape += [jax.ShapeDtypeStruct((rows, 2 * cols), jnp.bfloat16)] * 2
        scratch = [pltpu.VMEM((held, BS, cols), jnp.float32)] * 2
    scratch += [pltpu.VMEM((held, BS, cols), jnp.bfloat16)] * 2
    return pl.pallas_call(
        functools.partial(backward_kernel, own),
        grid_spec=pltpu.PrefetchScalarGridSpec(
            num_scalar_prefetch=3,
            grid=(blocks // TWO,),
            in_specs=in_specs,
            out_specs=out_specs,
            scratch_shapes=scratch,
        ),
        out_shape=out_shape,
        compiler_params=pltpu.CompilerParams(dimension_semantics=("arbitrary",)),
        cost_estimate=cost(blocks),
        name="backward",
    )(*tables, query_rows, grad_attended, att_t, stats, keys_t, *sources, *base)


def shifted(x, axis, by):
    count = lax.axis_size(axis)
    return lax.ppermute(x, axis, [(i, (i + by) % count) for i in range(count)])


def project_kernel(g_ref, w_ref, att_ref, ga_ref, wg_ref):
    count = g_ref.shape[0]
    att = att_ref[...]
    total = None
    for k in range(0, count, 2):
        part = jnp.concatenate([g_ref[k], g_ref[k + 1]], axis=1)
        side = w_ref[:, k * BS : (k + 2) * BS]
        term = lax.dot_general(
            part, side, (((1,), (1,)), ((), ())), preferred_element_type=jnp.float32
        )
        total = term if total is None else total + term
        grad = dot(att, part)
        for j in range(2):
            wg_ref[k + j] = grad[:, j * BS : (j + 1) * BS].astype(wg_ref.dtype)
    ga_ref[...] = total.astype(jnp.bfloat16)


def project(gathered, out_weight, att_t):
    count, rows, width = gathered.shape
    cols = out_weight.shape[0]
    return pl.pallas_call(
        project_kernel,
        in_specs=[pl.BlockSpec(memory_space=pltpu.VMEM)] * 3,
        out_shape=[
            jax.ShapeDtypeStruct((rows, cols), jnp.bfloat16),
            jax.ShapeDtypeStruct((count, cols, width), jnp.bfloat16),
        ],
        cost_estimate=cost(2),
        name="project",
    )(gathered, out_weight, att_t)


def place_kernel(sum_ref, out_ref):
    for k in range(sum_ref.shape[0]):
        out_ref[:, k * BS : (k + 1) * BS] = sum_ref[k].astype(jnp.float32)


def place(sums):
    count, cols, width = sums.shape
    return pl.pallas_call(
        place_kernel,
        out_shape=jax.ShapeDtypeStruct((cols, count * width), jnp.float32),
        name="place",
    )(sums)


def gather_heads(rows):
    copies = jnp.broadcast_to(rows[None], (lax.axis_size("head"),) + rows.shape)
    return lax.all_to_all(copies, "head", 0, 0)


def slot_tables(neighbours, counts, blocks):
    first = lax.axis_index("ctx") * blocks
    places = lax.dynamic_slice_in_dim(neighbours, first, blocks, axis=0)
    places = jnp.clip(places - (first - blocks), 0, 3 * blocks - 1)
    active = lax.dynamic_slice_in_dim(counts, first, blocks, axis=0)
    slots = jnp.arange(places.shape[1], dtype=jnp.int32)
    own = (places >= blocks) & (places < 2 * blocks)
    kind = jnp.where(slots < active[:, None], own.astype(jnp.int32), 2)
    key = kind * places.shape[1] + slots
    rank = jnp.sum((key[:, :, None] > key[:, None, :]).astype(jnp.int32), axis=2)
    chosen = rank[:, :, None] == slots
    ordered = jnp.sum(jnp.where(chosen, places[:, :, None], 0), axis=1)
    halo = jnp.sum((kind == 0).astype(jnp.int32), axis=1)
    return ordered, active, halo


def body(query_rows, key_rows, value_rows, out_grad, out_weight, neighbours, counts):
    row_count, col_count = query_rows.shape
    blocks = row_count // BS
    node_count = row_count * lax.axis_size("ctx")
    gathered = gather_heads(out_grad)
    packed = jnp.concatenate([key_rows, value_rows], axis=1)
    left = shifted(packed, "ctx", 1)
    right = shifted(packed, "ctx", -1)
    tables = slot_tables(neighbours, counts, blocks)
    att_t, stats, keys_t = forward(*tables[:2], query_rows, key_rows, value_rows, left, right)
    grad_attended, partial = project(gathered, out_weight, att_t)
    shared = (query_rows, grad_attended, att_t, stats, keys_t)
    members = lax.axis_size("ctx")
    pieces = partial.reshape(members, -1, partial.shape[-1])
    pieces = lax.all_to_all(pieces, "ctx", 0, 0)
    query_part, to_left, to_right = backward(tables, *shared, (left, right), ())
    from_right = shifted(to_left, "ctx", -1)
    from_left = shifted(to_right, "ctx", 1)
    piece = jnp.sum(pieces.astype(jnp.float32), axis=0) * node_count ** (-0.5)
    copies = jnp.broadcast_to(piece.astype(partial.dtype)[None], pieces.shape)
    weight_sum = lax.all_to_all(copies, "ctx", 0, 0)
    query_grad, key_own, value_own = backward(
        tables, *shared, (key_rows, value_rows), (query_part,)
    )
    weight_grad = place(weight_sum.reshape(partial.shape))
    sides = [
        own.reshape(row_count, col_count)
        + from_right[:, at : at + col_count].astype(jnp.float32)
        + from_left[:, at : at + col_count].astype(jnp.float32)
        for own, at in ((key_own, 0), (value_own, col_count))
    ]
    key_grad, value_grad = [side.astype(jnp.bfloat16) for side in sides]
    return (query_grad, key_grad, value_grad, weight_grad)


def solution(mesh):
    placed = (
        P("ctx", "head"),
        P("ctx", "head"),
        P("ctx", "head"),
        P("ctx", "head"),
        P("head", None),
        P(),
        P(),
    )
    return jax.shard_map(
        body,
        mesh=mesh,
        in_specs=placed,
        out_specs=(P("ctx", "head"), P("ctx", "head"), P("ctx", "head"), P("head", None)),
        check_vma=False,
    )
```
